32 devices in a mesh: member: 4 (over y, core), space: 8 (over z, x).
Axes of the slice: x: 2, y: 2, z: 4, core: 2. Of those that a mesh axis runs over, the one named last changes fastest.
Arguments:
- prior_sample: float32 [256, 65536], P('member', 'space'), may hold values from -6 to 6
- measured_point_location: int32 [32, 128], P('space'), may hold values from 0 to 8191
- measured_data: float32 [32, 128], P('space'), may hold values from -12 to 12
- measurement_noise_sigma: float32 [32, 128], P('space'), may hold values from 2 to 64
- measured_slots_used: int32 [8], P('space'), may hold values from 128 to 512, as said below
Outputs:
- analysis: float32 [256, 65536], P('member', 'space')
The draws below stay inside these ranges and needn't reach their ends.
Inputs may be any that keep to these rules, and one draw needn't show every extreme that they name: measured_slots_used gives for each space block how many of its first slots are in use; some block uses all 512 slots. `measured_point_location`: each index is a state point of the observation's own space block.
All inputs are finite; a program needn't handle non-finite values.
Results may differ from the reference program's by a relative error of at most 0.000088.
Values sent between devices are 32-bit elements; how exact they have to be, the bound alone decides.
A program may use at most 64 MiB of HBM per device.

```python
import math
import jax
import jax.numpy as jnp
from jax import lax

SAMPLE_TOTAL = 256
ROW = 128
POINTS_IN_REGION = 8192
REGION_TOTAL = 8
GRID_POINTS = 65536
OBS_BLK = 512
OBS_ROWS = 32


def draw_measured_slots_used(key, part):
    counts = jax.random.randint(key, (REGION_TOTAL,), OBS_BLK // 4, OBS_BLK + 1)
    chosen = jax.random.randint(jax.random.fold_in(key, 7), (), 0, REGION_TOTAL)
    full_block = jnp.arange(REGION_TOTAL) == chosen
    return jnp.where(full_block, OBS_BLK, counts).astype(jnp.int32)


def touch_ends(array, own_key, low, top_value):
    shape = array.shape
    index_at = [jax.random.randint(jax.random.fold_in(own_key, axis), (), 0, shape[axis]) for axis in range(len(shape))]
    array = array.at[tuple(index_at)].set(low)
    longest = shape.index(max(shape))
    index_at[longest] = (index_at[longest] + 1) % shape[longest]
    return array.at[tuple(index_at)].set(top_value)


def block_levels(key, shape, split, least, high):
    def one(position, blocks):
        draws = jax.random.uniform(jax.random.fold_in(jax.random.fold_in(key, 6), position), (blocks,), jnp.float32, least / len(split), high / len(split))
        return jnp.repeat(jnp.exp(draws), shape[position] // blocks).reshape((-1,) + (1,) * (len(shape) - position - 1))

    factor_of = one(*split[0])
    for cut in split[1:]:
        factor_of = factor_of * one(*cut)
    return factor_of


def bell_draw(rng, shape, width, limit, shards=(), kind=jnp.bfloat16):
    entries = jax.random.normal(rng, shape, jnp.float32) * width
    if len(shards) > 0:
        entries = block_levels(rng, shape, shards, -0.22, 0.18) * entries
    return jnp.clip(entries, min=-limit, max=limit).astype(kind)


def setup_inputs(seed: int = 0) -> dict:
    key_list = jax.random.split(jax.random.key(seed), 6)
    prior_sample = bell_draw(key_list[0], (SAMPLE_TOTAL, GRID_POINTS), 1.0, 6.0, ((0, 4), (1, 8)), jnp.float32)
    measured_point_location = touch_ends(jax.random.randint(key_list[1], (OBS_ROWS, ROW), 0, POINTS_IN_REGION), jax.random.fold_in(key_list[1], 1), 0, POINTS_IN_REGION - 1).astype(jnp.int32)
    measured_data = bell_draw(key_list[2], (OBS_ROWS, ROW), 3.0, 12.0, ((0, 8),), jnp.float32)
    measurement_noise_sigma = jnp.clip(jnp.exp(math.log(64.0) - 3.465736 * jax.random.uniform(key_list[3], (OBS_ROWS, ROW), jnp.float32) ** block_levels(key_list[3], (OBS_ROWS, ROW), ((0, 8),), -0.2, 0.2)), 2.0, 64.0)
    measured_slots_used = draw_measured_slots_used(jax.random.fold_in(key_list[5], 71), 0)
    return {"prior_sample": prior_sample, "measured_point_location": measured_point_location, "measured_data": measured_data, "measurement_noise_sigma": measurement_noise_sigma, "measured_slots_used": measured_slots_used}


def lower_inverse(lower_factor):
    size_k = lower_factor.shape[0]
    ident = jnp.eye(size_k, dtype=lower_factor.dtype)
    return lax.linalg.triangular_solve(lower_factor, ident, left_side=True, lower=True)

def reference(prior_sample, measured_point_location, measured_data, measurement_noise_sigma, measured_slots_used):
    exact_arithmetic = lax.Precision.HIGHEST
    sample_total = prior_sample.shape[0]
    region_total = prior_sample.reshape(sample_total, REGION_TOTAL, POINTS_IN_REGION)
    index_blocks = measured_point_location.reshape(REGION_TOTAL, OBS_BLK)
    propagated_grid = jax.vmap(lambda block, places: jnp.take(block, places, axis=1), in_axes=(1, 0), out_axes=1)(region_total, index_blocks)
    propagated_grid = propagated_grid.reshape(sample_total, REGION_TOTAL * OBS_BLK)
    slots = jnp.arange(OBS_BLK, dtype=jnp.int32)
    valid = (slots[None, :] < measured_slots_used[:, None]).reshape(-1)
    weight = jnp.where(valid, 1.0 / measurement_noise_sigma.reshape(-1), jnp.zeros_like(measurement_noise_sigma.reshape(-1)))
    sim_mean = lax.optimization_barrier(jnp.mean(propagated_grid, axis=0))
    perturbed = (propagated_grid - sim_mean[None, :]) * weight[None, :]
    innovation = (measured_data.reshape(-1) - sim_mean) * weight
    gram_all = jnp.dot(perturbed, perturbed.T, precision=exact_arithmetic)
    cross = jnp.dot(perturbed, innovation, precision=exact_arithmetic)
    cov_matrix = gram_all + (sample_total - 1) * jnp.eye(sample_total, dtype=gram_all.dtype)
    lower_factor = jnp.linalg.cholesky(cov_matrix)
    inverse = lower_inverse(lower_factor)
    projected = jnp.dot(inverse, cross, precision=exact_arithmetic)
    mean_weight = jnp.dot(inverse.T, projected, precision=exact_arithmetic)
    weight_matrix_update = math.sqrt(sample_total - 1) * inverse + mean_weight[None, :]
    prior_average = lax.optimization_barrier(jnp.mean(prior_sample, axis=0))
    return prior_average[None, :] + jnp.dot(weight_matrix_update, prior_sample - prior_average[None, :], precision=exact_arithmetic)
```

```python
import functools
import math

import jax
import jax.numpy as jnp
from jax import lax
from jax.experimental import pallas as pl
from jax.experimental.pallas import tpu as pltpu
from jax.sharding import PartitionSpec as P


def solve_lower(lower_factor, target):
    return lax.linalg.triangular_solve(lower_factor, target, left_side=True, lower=True)


def general_body(
    prior_sample,
    measured_point_location,
    measured_data,
    measurement_noise_sigma,
    measured_slots_used,
):
    exact_arithmetic = lax.Precision.HIGHEST
    anomaly_matrix, points_in_region = prior_sample.shape
    region_batches = lax.axis_size("member")
    sample_total = anomaly_matrix * region_batches
    pointwise_spread = points_in_region // region_batches
    linear_position = measured_point_location.reshape(-1)
    obs_blk = linear_position.shape[0]
    observation_deviation = obs_blk // region_batches
    propagated_grid = jnp.take(prior_sample, linear_position, axis=1).reshape(
        anomaly_matrix, region_batches, observation_deviation
    )
    prior_regions = prior_sample.reshape(anomaly_matrix, region_batches, pointwise_spread)
    prior_sample_full, integrate_dynamics = (
        lax.all_to_all(prior_regions, "member", split_axis=1, concat_axis=0, tiled=True),
        lax.all_to_all(propagated_grid, "member", split_axis=1, concat_axis=0, tiled=True),
    )
    integrate_dynamics = integrate_dynamics.reshape(sample_total, observation_deviation)
    rank = lax.axis_index("member")
    start = rank * observation_deviation
    my_value = lax.dynamic_slice_in_dim(measured_data.reshape(-1), start, observation_deviation)
    my_sigma = lax.dynamic_slice_in_dim(
        measurement_noise_sigma.reshape(-1), start, observation_deviation
    )
    slots = start + jnp.arange(observation_deviation, dtype=jnp.int32)
    valid = slots < measured_slots_used[0]
    weight = jnp.where(valid, 1.0 / my_sigma, jnp.zeros_like(my_sigma))
    sim_mean = jnp.mean(integrate_dynamics, axis=0)
    perturbed = (integrate_dynamics - sim_mean[None, :]) * weight[None, :]
    innovation = (my_value - sim_mean) * weight
    gram_loc = jnp.dot(perturbed, perturbed.T, precision=exact_arithmetic)
    cross_loc = jnp.dot(perturbed, innovation, precision=exact_arithmetic)
    gram_block, cross_block = lax.psum((gram_loc, cross_loc), "member")
    gram_all, cross = lax.psum((gram_block, cross_block), "space")
    cov_matrix = gram_all + (sample_total - 1) * jnp.eye(sample_total, dtype=jnp.float32)
    lower_factor = jnp.linalg.cholesky(cov_matrix)
    inverse = solve_lower(lower_factor, jnp.eye(sample_total, dtype=jnp.float32))
    projected = jnp.dot(inverse, cross, precision=exact_arithmetic)
    mean_weight = jnp.dot(inverse.T, projected, precision=exact_arithmetic)
    weight_matrix_update = math.sqrt(sample_total - 1) * inverse + mean_weight[None, :]
    sample_vectors = prior_sample_full.reshape(sample_total, -1)
    prior_average = jnp.mean(sample_vectors, axis=0)
    updated_sample = prior_average[None, :] + jnp.dot(
        weight_matrix_update, sample_vectors - prior_average[None, :], precision=exact_arithmetic
    )
    returned = lax.all_to_all(
        updated_sample.reshape(prior_sample_full.shape),
        "member",
        split_axis=0,
        concat_axis=1,
        tiled=True,
    )
    return returned.reshape(anomaly_matrix, points_in_region)


MESH = pl.DeviceIdType.MESH
VMEM_SPEC = pl.BlockSpec(memory_space=pltpu.VMEM)
LANES = 128
SUBLANES = 8


def split2(x):
    high = x.astype(jnp.bfloat16)
    low = (x - high.astype(jnp.float32)).astype(jnp.bfloat16)
    return high, low


def dot3(a, b, dims=((1,), (0,))):
    ah, al = split2(a)
    bh, bl = split2(b)
    d = functools.partial(
        lax.dot_general, dimension_numbers=(dims, ((), ())), preferred_element_type=jnp.float32
    )
    return (d(ah, bl) + d(al, bh)) + d(ah, bh)


def gather_kernel(x_ref, idx_ref, out_ref, acc_ref):
    step = pl.program_id(0)
    members, points = x_ref.shape
    slots = out_ref.shape[1]
    x = x_ref[...]
    high, rest = x.astype(jnp.bfloat16), None
    rest = x - high.astype(jnp.float32)
    mid = rest.astype(jnp.bfloat16)
    low = (rest - mid.astype(jnp.float32)).astype(jnp.bfloat16)
    parts = jnp.concatenate([high, mid, low], axis=0)
    index = jnp.concatenate([idx_ref[i : i + 1, :] for i in range(idx_ref.shape[0])], axis=1)
    where = lax.broadcasted_iota(jnp.int32, (points, slots), 0) + step * points
    hot = (where == index).astype(jnp.float32).astype(jnp.bfloat16)
    got = jnp.dot(parts, hot, preferred_element_type=jnp.float32)

    @pl.when(step == 0)
    def _():
        acc_ref[...] = got

    @pl.when(step > 0)
    def _():
        acc_ref[...] += got

    @pl.when(step == pl.num_programs(0) - 1)
    def _():
        total = acc_ref[...]
        out_ref[...] = (total[:members] + total[members : 2 * members]) + total[2 * members :]


def gather_observed(prior, index, tile=1024):
    members, points = prior.shape
    slots = index.size
    return pl.pallas_call(
        gather_kernel,
        grid=(points // tile,),
        out_shape=jax.ShapeDtypeStruct((members, slots), jnp.float32),
        in_specs=[
            pl.BlockSpec((members, tile), lambda i: (0, i)),
            pl.BlockSpec(index.shape, lambda i: (0, 0)),
        ],
        out_specs=pl.BlockSpec((members, slots), lambda i: (0, 0)),
        scratch_shapes=[pltpu.VMEM((3 * members, slots), jnp.float32)],
    )(prior, index)


def flat_row(ref):
    return jnp.concatenate([ref[i : i + 1, :] for i in range(ref.shape[0])], axis=1)


def gram_kernel(
    spaces,
    ev_ref,
    data_ref,
    sigma_ref,
    used_ref,
    out_ref,
    ev_all,
    gram,
    parts,
    total,
    ex_send,
    ex_recv,
    rs_send,
    rs_recv,
    ag_send,
    ag_recv,
    fin_send,
    fin_recv,
):
    rank = lax.axis_index("member")
    place = lax.axis_index("space")
    rows, slots = ev_ref.shape
    samples = ev_all.shape[0]
    chunk = rows // spaces
    side = rank + 1 - 2 * lax.rem(rank, 2)
    across = lax.rem(rank + 2, 4)

    barrier = pltpu.get_barrier_semaphore()
    for other in (side, across):
        pl.semaphore_signal(
            barrier, inc=1, device_id={"member": other, "space": place}, device_id_type=MESH
        )
    for d in range(1, spaces):
        pl.semaphore_signal(
            barrier,
            inc=1,
            device_id={"member": rank, "space": lax.rem(place + d, spaces)},
            device_id_type=MESH,
        )
    pl.semaphore_wait(barrier, spaces + 1)

    def send(src, dst, ssem, rsem, member, space):
        copy = pltpu.make_async_remote_copy(
            src_ref=src,
            dst_ref=dst,
            send_sem=ssem,
            recv_sem=rsem,
            device_id={"member": member, "space": space},
            device_id_type=MESH,
        )
        copy.start()
        return copy

    def member_rows(ref, member):
        return ref.at[pl.ds(pl.multiple_of(member * rows, SUBLANES), rows)]

    def exchange(source, full, ssem, rsem):
        far = send(source, member_rows(full, rank), ssem.at[0], rsem.at[0], across, place)
        near = send(source, member_rows(full, rank), ssem.at[1], rsem.at[1], side, place)
        far.wait_recv()
        got = member_rows(full, across)
        relay = send(got, got, ssem.at[2], rsem.at[2], side, place)
        near.wait_recv()
        relay.wait_recv()
        return (far, near, relay)

    pending = exchange(ev_ref, ev_all, ex_send, ex_recv)
    own = pl.ds(pl.multiple_of(rank * rows, SUBLANES), rows)
    ev_all[own, :] = ev_ref[...]

    slot = lax.broadcasted_iota(jnp.int32, (1, slots), 1)
    weight = jnp.where(slot < used_ref[0], 1.0 / flat_row(sigma_ref), 0.0)
    ev = ev_all[...]
    mean = jnp.sum(ev, axis=0, keepdims=True) * (1.0 / samples)
    anomalies = (ev - mean) * weight
    innovation = (flat_row(data_ref) - mean) * weight
    first = lax.broadcasted_iota(jnp.int32, (LANES, slots), 0) == 0
    extra = jnp.where(first, jnp.broadcast_to(innovation, (LANES, slots)), 0.0)
    mine = (ev_ref[...] - mean) * weight
    right = jnp.concatenate([anomalies, extra], axis=0)
    gram[...] = dot3(mine, right, ((1,), (1,)))

    copies = []
    for d in range(1, spaces):
        other = lax.rem(place + d, spaces)
        copies.append(
            send(
                gram.at[pl.ds(pl.multiple_of(other * chunk, SUBLANES), chunk)],
                parts.at[d - 1],
                rs_send.at[d - 1],
                rs_recv.at[d - 1],
                rank,
                other,
            )
        )
    acc = gram[pl.ds(pl.multiple_of(place * chunk, SUBLANES), chunk), :]
    for d in range(1, spaces):
        copies[d - 1].wait_recv()
        acc = acc + parts[d - 1]
    piece = pl.ds(pl.multiple_of(rank * rows + place * chunk, SUBLANES), chunk)
    total[piece, :] = acc
    spread = []
    for d in range(1, spaces):
        other = lax.rem(place + d, spaces)
        spread.append(
            send(
                total.at[piece], total.at[piece], ag_send.at[d - 1], ag_recv.at[d - 1], rank, other
            )
        )
    for copy in spread:
        copy.wait_recv()
    last = exchange(member_rows(total, rank), total, fin_send, fin_recv)
    for copy in (*pending, *copies, *spread, *last):
        copy.wait_send()
    out_ref[...] = total[...]


def summed_gram(ev, data, sigma, used, members, spaces):
    rows, slots = ev.shape
    samples = rows * members
    width = samples + LANES
    dma = pltpu.SemaphoreType.DMA
    return pl.pallas_call(
        functools.partial(gram_kernel, spaces),
        out_shape=jax.ShapeDtypeStruct((samples, width), jnp.float32),
        in_specs=[VMEM_SPEC] * 3 + [pl.BlockSpec(memory_space=pltpu.SMEM)],
        out_specs=VMEM_SPEC,
        scratch_shapes=[
            pltpu.VMEM((samples, slots), jnp.float32),
            pltpu.VMEM((rows, width), jnp.float32),
            pltpu.VMEM((spaces - 1, rows // spaces, width), jnp.float32),
            pltpu.VMEM((samples, width), jnp.float32),
            dma((3,)),
            dma((3,)),
            dma((spaces - 1,)),
            dma((spaces - 1,)),
            dma((spaces - 1,)),
            dma((spaces - 1,)),
            dma((3,)),
            dma((3,)),
        ],
        compiler_params=pltpu.CompilerParams(collective_id=0, has_side_effects=True),
    )(ev, data, sigma, used)


PIVOTS = 4


def inverse_factor(a):
    size = a.shape[0]
    count = size // SUBLANES
    shape = (SUBLANES, size)
    m = [a[SUBLANES * i : SUBLANES * (i + 1), :] for i in range(count)]
    diag = [None] * count
    lane = lax.broadcasted_iota(jnp.int32, shape, 1)
    sub = lax.broadcasted_iota(jnp.int32, shape, 0)

    def column(x, k):
        return jnp.broadcast_to(x[:, k : k + 1], shape)

    def row(x, r):
        return jnp.broadcast_to(x[r : r + 1, :], shape)

    for k in range(0, size, PIVOTS):
        t, r = divmod(k, SUBLANES)
        inside = (lane >= k) & (lane < k + PIVOTS)
        cols = [column(m[t], k + q) for q in range(PIVOTS)]
        pivot = {(q, p): row(cols[p], r + q) for p in range(PIVOTS) for q in range(p, PIVOTS)}
        base = [
            jnp.where(inside, jnp.where(lane == k + q, 1.0, 0.0), row(m[t], r + q))
            for q in range(PIVOTS)
        ]
        inverse = []
        for p in range(PIVOTS):
            inverse.append(1.0 / pivot[p, p])
            for q in range(p + 1, PIVOTS):
                factor = pivot[q, p] * inverse[p]
                base[q] = base[q] - factor * base[p]
                for s in range(q, PIVOTS):
                    pivot[s, q] = pivot[s, q] - factor * pivot[s, p]
        for p in range(PIVOTS):
            old = diag[t]
            diag[t] = pivot[p, p] if old is None else jnp.where(sub >= r + p, pivot[p, p], old)
        for i in range(t, count):
            cols_i = cols if i == t else [column(m[i], k + q) for q in range(PIVOTS)]
            cols_i = list(cols_i)
            if i == t:
                unit = jnp.where(lane - k == sub - r, 1.0, 0.0)
                x = jnp.where(inside & (sub >= r), unit, m[i])
            else:
                x = jnp.where(inside, 0.0, m[i])
            for p in range(PIVOTS):
                mult = cols_i[p] * inverse[p]
                if i == t:
                    mult = jnp.where(sub > r + p, mult, 0.0)
                for q in range(p + 1, PIVOTS):
                    cols_i[q] = cols_i[q] - mult * pivot[q, p]
                x = x - mult * base[p]
            m[i] = x
    out = []
    for i in range(count):
        keep = lane <= sub + SUBLANES * i
        out.append(jnp.where(keep, m[i] * lax.rsqrt(diag[i]), 0.0))
    return jnp.concatenate(out, axis=0)


def eye_mask(rows, cols):
    shape = (rows, cols)
    return lax.broadcasted_iota(jnp.int32, shape, 0) == lax.broadcasted_iota(jnp.int32, shape, 1)


def transform_kernel(g_ref, out_ref, inv_ref):
    samples = g_ref.shape[0]
    b = LANES
    ridge = float(samples - 1)
    n = samples // b
    work = {}
    for i in range(n):
        for j in range(i + 1):
            block = g_ref[i * b : (i + 1) * b, j * b : (j + 1) * b]
            work[i, j] = block + jnp.where(eye_mask(b, b), ridge, 0.0) if i == j else block
    inv = {}
    low = {}
    for k in range(n):
        inv[k, k] = inverse_factor(work[k, k])
        for i in range(k + 1, n):
            low[i, k] = dot3(work[i, k], inv[k, k], ((1,), (1,)))
        for i in range(k + 1, n):
            for j in range(k + 1, i + 1):
                work[i, j] = work[i, j] - dot3(low[i, k], low[j, k], ((1,), (1,)))
        for j in range(k):
            acc = dot3(low[k, j], inv[j, j])
            for s in range(j + 1, k):
                acc = acc + dot3(low[k, s], inv[s, j])
            inv[k, j] = -dot3(inv[k, k], acc)
    zero = jnp.zeros((b, b), jnp.float32)
    full = jnp.concatenate(
        [
            jnp.concatenate([inv[i, j] if j <= i else zero for j in range(n)], axis=1)
            for i in range(n)
        ],
        axis=0,
    )
    inv_ref[...] = full
    cross = g_ref[:, samples : samples + b]
    projected = dot3(full, cross)
    mean_weight = jnp.sum(full * projected[:, 0:1], axis=0, keepdims=True)
    out_ref[...] = math.sqrt(samples - 1) * full + mean_weight


def transform_of(gram):
    samples = gram.shape[0]
    return pl.pallas_call(
        transform_kernel,
        out_shape=jax.ShapeDtypeStruct((samples, samples), jnp.float32),
        in_specs=[VMEM_SPEC],
        out_specs=VMEM_SPEC,
        scratch_shapes=[pltpu.VMEM((samples, samples), jnp.float32)],
        cost_estimate=pl.CostEstimate(
            flops=40_000_000, bytes_accessed=4 * samples * samples * 40, transcendentals=0
        ),
    )(gram)


def analysis_kernel(t_ref, own_ref, side_ref, across_ref, both_ref, out_ref, x_ref):
    rank = lax.axis_index("member")
    rows = own_ref.shape[0]
    samples = x_ref.shape[0]
    side = rank + 1 - 2 * lax.rem(rank, 2)
    across = lax.rem(rank + 2, 4)
    both = lax.rem(side + 2, 4)
    pieces = ((rank, own_ref), (side, side_ref), (across, across_ref), (both, both_ref))
    total = None
    for member, ref in pieces:
        part = jnp.sum(ref[...], axis=0, keepdims=True)
        total = part if total is None else total + part
    mean = total * (1.0 / samples)
    for member, ref in pieces:
        x_ref[pl.ds(pl.multiple_of(member * rows, SUBLANES), rows), :] = ref[...] - mean
    mine = t_ref[pl.ds(pl.multiple_of(rank * rows, SUBLANES), rows), :]
    out_ref[...] = mean + dot3(mine, x_ref[...])


def analysis_rows(transform, pieces, tile=1024):
    rows, points = pieces[0].shape
    samples = transform.shape[0]
    block = pl.BlockSpec((rows, tile), lambda i: (0, i))
    return pl.pallas_call(
        analysis_kernel,
        grid=(points // tile,),
        out_shape=jax.ShapeDtypeStruct((rows, points), jnp.float32),
        in_specs=[pl.BlockSpec((samples, samples), lambda i: (0, 0))] + [block] * 4,
        out_specs=block,
        scratch_shapes=[pltpu.VMEM((samples, tile), jnp.float32)],
    )(transform, *pieces)


def body(prior_sample, location, data, sigma, used):
    rows, points = prior_sample.shape
    members = lax.axis_size("member")
    spaces = lax.axis_size("space")
    if members != 4 or rows % (SUBLANES * spaces) or (rows * members) % LANES:
        return general_body(prior_sample, location, data, sigma, used)
    near = [(i, i ^ 1) for i in range(members)]
    far = [(i, i ^ 2) for i in range(members)]
    across = lax.ppermute(prior_sample, "member", far)
    side = lax.ppermute(prior_sample, "member", near)
    both = lax.ppermute(across, "member", near)
    observed = gather_observed(prior_sample, location)
    gram = summed_gram(observed, data, sigma, used, members, spaces)
    transform = transform_of(gram)
    return analysis_rows(transform, (prior_sample, side, across, both))


def solution(mesh):
    placed = (
        P("member", "space"),
        P("space", None),
        P("space", None),
        P("space", None),
        P("space"),
    )
    return jax.shard_map(
        body, mesh=mesh, in_specs=placed, out_specs=P("member", "space"), check_vma=False
    )
```

```python
import functools
import math

import jax
import jax.numpy as jnp
from jax import lax
from jax.experimental import pallas as pl
from jax.experimental.pallas import tpu as pltpu
from jax.sharding import PartitionSpec as P


def solve_lower(lower_factor, target):
    return lax.linalg.triangular_solve(lower_factor, target, left_side=True, lower=True)


def general_body(
    prior_sample,
    measured_point_location,
    measured_data,
    measurement_noise_sigma,
    measured_slots_used,
):
    exact_arithmetic = lax.Precision.HIGHEST
    anomaly_matrix, points_in_region = prior_sample.shape
    region_batches = lax.axis_size("member")
    sample_total = anomaly_matrix * region_batches
    pointwise_spread = points_in_region // region_batches
    linear_position = measured_point_location.reshape(-1)
    obs_blk = linear_position.shape[0]
    observation_deviation = obs_blk // region_batches
    propagated_grid = jnp.take(prior_sample, linear_position, axis=1).reshape(
        anomaly_matrix, region_batches, observation_deviation
    )
    prior_regions = prior_sample.reshape(anomaly_matrix, region_batches, pointwise_spread)
    prior_sample_full, integrate_dynamics = (
        lax.all_to_all(prior_regions, "member", split_axis=1, concat_axis=0, tiled=True),
        lax.all_to_all(propagated_grid, "member", split_axis=1, concat_axis=0, tiled=True),
    )
    integrate_dynamics = integrate_dynamics.reshape(sample_total, observation_deviation)
    rank = lax.axis_index("member")
    start = rank * observation_deviation
    my_value = lax.dynamic_slice_in_dim(measured_data.reshape(-1), start, observation_deviation)
    my_sigma = lax.dynamic_slice_in_dim(
        measurement_noise_sigma.reshape(-1), start, observation_deviation
    )
    slots = start + jnp.arange(observation_deviation, dtype=jnp.int32)
    valid = slots < measured_slots_used[0]
    weight = jnp.where(valid, 1.0 / my_sigma, jnp.zeros_like(my_sigma))
    sim_mean = jnp.mean(integrate_dynamics, axis=0)
    perturbed = (integrate_dynamics - sim_mean[None, :]) * weight[None, :]
    innovation = (my_value - sim_mean) * weight
    gram_loc = jnp.dot(perturbed, perturbed.T, precision=exact_arithmetic)
    cross_loc = jnp.dot(perturbed, innovation, precision=exact_arithmetic)
    gram_block, cross_block = lax.psum((gram_loc, cross_loc), "member")
    gram_all, cross = lax.psum((gram_block, cross_block), "space")
    cov_matrix = gram_all + (sample_total - 1) * jnp.eye(sample_total, dtype=jnp.float32)
    lower_factor = jnp.linalg.cholesky(cov_matrix)
    inverse = solve_lower(lower_factor, jnp.eye(sample_total, dtype=jnp.float32))
    projected = jnp.dot(inverse, cross, precision=exact_arithmetic)
    mean_weight = jnp.dot(inverse.T, projected, precision=exact_arithmetic)
    weight_matrix_update = math.sqrt(sample_total - 1) * inverse + mean_weight[None, :]
    sample_vectors = prior_sample_full.reshape(sample_total, -1)
    prior_average = jnp.mean(sample_vectors, axis=0)
    updated_sample = prior_average[None, :] + jnp.dot(
        weight_matrix_update, sample_vectors - prior_average[None, :], precision=exact_arithmetic
    )
    returned = lax.all_to_all(
        updated_sample.reshape(prior_sample_full.shape),
        "member",
        split_axis=0,
        concat_axis=1,
        tiled=True,
    )
    return returned.reshape(anomaly_matrix, points_in_region)


MESH = pl.DeviceIdType.MESH
VMEM_SPEC = pl.BlockSpec(memory_space=pltpu.VMEM)
LANES = 128
SUBLANES = 8


def split2(x):
    high = x.astype(jnp.bfloat16)
    low = (x - high.astype(jnp.float32)).astype(jnp.bfloat16)
    return high, low


def dot3(a, b, dims=((1,), (0,))):
    ah, al = split2(a)
    bh, bl = split2(b)
    d = functools.partial(
        lax.dot_general, dimension_numbers=(dims, ((), ())), preferred_element_type=jnp.float32
    )
    return (d(ah, bl) + d(al, bh)) + d(ah, bh)


def flat_row(ref):
    return jnp.concatenate([ref[i : i + 1, :] for i in range(ref.shape[0])], axis=1)


def gather_kernel(x_ref, idx_ref, out_ref):
    step = pl.program_id(0)
    members, points = x_ref.shape
    shape = (SUBLANES, LANES)
    for c in range(idx_ref.shape[0]):
        index = jnp.broadcast_to(idx_ref[c : c + 1, :], shape)
        lane = jnp.bitwise_and(index, LANES - 1)
        block = jnp.right_shift(index, LANES.bit_length() - 1) - step * (points // LANES)
        hits = [block == j for j in range(points // LANES)]
        columns = slice(c * LANES, (c + 1) * LANES)
        for g in range(0, members, SUBLANES):
            old = out_ref[g : g + SUBLANES, columns]
            got = jnp.where(step == 0, jnp.zeros(shape, jnp.float32), old)
            for j in range(points // LANES):
                x = x_ref[g : g + SUBLANES, j * LANES : (j + 1) * LANES]
                got = jnp.where(hits[j], jnp.take_along_axis(x, lane, axis=1), got)
            out_ref[g : g + SUBLANES, columns] = got


def gather_observed(prior, index, tile=2048):
    members, points = prior.shape
    slots = index.size
    return pl.pallas_call(
        gather_kernel,
        grid=(points // tile,),
        out_shape=jax.ShapeDtypeStruct((members, slots), jnp.float32),
        in_specs=[
            pl.BlockSpec((members, tile), lambda i: (0, i)),
            pl.BlockSpec(index.shape, lambda i: (0, 0)),
        ],
        out_specs=pl.BlockSpec((members, slots), lambda i: (0, 0)),
        cost_estimate=pl.CostEstimate(
            flops=2 * members * slots * 256, bytes_accessed=16_000_000, transcendentals=0
        ),
    )(prior, index)


def gram_kernel(
    spaces,
    ev_ref,
    data_ref,
    sigma_ref,
    used_ref,
    out_ref,
    ev_all,
    gram,
    parts,
    total,
    ex_send,
    ex_recv,
    rs_send,
    rs_recv,
    ag_send,
    ag_recv,
    fin_send,
    fin_recv,
):
    rank = lax.axis_index("member")
    place = lax.axis_index("space")
    rows, slots = ev_ref.shape
    samples = ev_all.shape[0]
    chunk = rows // spaces
    side = rank + 1 - 2 * lax.rem(rank, 2)
    across = lax.rem(rank + 2, 4)

    barrier = pltpu.get_barrier_semaphore()
    for other in (side, across):
        pl.semaphore_signal(
            barrier, inc=1, device_id={"member": other, "space": place}, device_id_type=MESH
        )
    for d in range(1, spaces):
        pl.semaphore_signal(
            barrier,
            inc=1,
            device_id={"member": rank, "space": lax.rem(place + d, spaces)},
            device_id_type=MESH,
        )
    pl.semaphore_wait(barrier, spaces + 1)

    def send(src, dst, ssem, rsem, member, space):
        copy = pltpu.make_async_remote_copy(
            src_ref=src,
            dst_ref=dst,
            send_sem=ssem,
            recv_sem=rsem,
            device_id={"member": member, "space": space},
            device_id_type=MESH,
        )
        copy.start()
        return copy

    def member_rows(ref, member):
        return ref.at[pl.ds(pl.multiple_of(member * rows, SUBLANES), rows)]

    def exchange(source, full, ssem, rsem):
        far = send(source, member_rows(full, rank), ssem.at[0], rsem.at[0], across, place)
        near = send(source, member_rows(full, rank), ssem.at[1], rsem.at[1], side, place)
        far.wait_recv()
        got = member_rows(full, across)
        relay = send(got, got, ssem.at[2], rsem.at[2], side, place)
        near.wait_recv()
        relay.wait_recv()
        return (far, near, relay)

    pending = exchange(ev_ref, ev_all, ex_send, ex_recv)
    own = pl.ds(pl.multiple_of(rank * rows, SUBLANES), rows)
    ev_all[own, :] = ev_ref[...]

    slot = lax.broadcasted_iota(jnp.int32, (1, slots), 1)
    weight = jnp.where(slot < used_ref[0], 1.0 / flat_row(sigma_ref), 0.0)
    ev = ev_all[...]
    mean = jnp.sum(ev, axis=0, keepdims=True) * (1.0 / samples)
    anomalies = (ev - mean) * weight
    innovation = (flat_row(data_ref) - mean) * weight
    first = lax.broadcasted_iota(jnp.int32, (LANES, slots), 0) == 0
    extra = jnp.where(first, jnp.broadcast_to(innovation, (LANES, slots)), 0.0)
    mine = (ev_ref[...] - mean) * weight
    right = jnp.concatenate([anomalies, extra], axis=0)
    gram[...] = dot3(mine, right, ((1,), (1,)))

    copies = []
    for d in range(1, spaces):
        other = lax.rem(place + d, spaces)
        copies.append(
            send(
                gram.at[pl.ds(pl.multiple_of(other * chunk, SUBLANES), chunk)],
                parts.at[d - 1],
                rs_send.at[d - 1],
                rs_recv.at[d - 1],
                rank,
                other,
            )
        )
    acc = gram[pl.ds(pl.multiple_of(place * chunk, SUBLANES), chunk), :]
    for d in range(1, spaces):
        copies[d - 1].wait_recv()
        acc = acc + parts[d - 1]
    piece = pl.ds(pl.multiple_of(rank * rows + place * chunk, SUBLANES), chunk)
    total[piece, :] = acc
    spread = []
    for d in range(1, spaces):
        other = lax.rem(place + d, spaces)
        spread.append(
            send(
                total.at[piece], total.at[piece], ag_send.at[d - 1], ag_recv.at[d - 1], rank, other
            )
        )
    for copy in spread:
        copy.wait_recv()
    last = exchange(member_rows(total, rank), total, fin_send, fin_recv)
    for copy in (*pending, *copies, *spread, *last):
        copy.wait_send()
    out_ref[...] = total[...]


def summed_gram(ev, data, sigma, used, members, spaces):
    rows, slots = ev.shape
    samples = rows * members
    width = samples + LANES
    dma = pltpu.SemaphoreType.DMA
    return pl.pallas_call(
        functools.partial(gram_kernel, spaces),
        out_shape=jax.ShapeDtypeStruct((samples, width), jnp.float32),
        in_specs=[VMEM_SPEC] * 3 + [pl.BlockSpec(memory_space=pltpu.SMEM)],
        out_specs=VMEM_SPEC,
        scratch_shapes=[
            pltpu.VMEM((samples, slots), jnp.float32),
            pltpu.VMEM((rows, width), jnp.float32),
            pltpu.VMEM((spaces - 1, rows // spaces, width), jnp.float32),
            pltpu.VMEM((samples, width), jnp.float32),
            dma((3,)),
            dma((3,)),
            dma((spaces - 1,)),
            dma((spaces - 1,)),
            dma((spaces - 1,)),
            dma((spaces - 1,)),
            dma((3,)),
            dma((3,)),
        ],
        compiler_params=pltpu.CompilerParams(collective_id=0, has_side_effects=True),
        cost_estimate=pl.CostEstimate(
            flops=40_000_000, bytes_accessed=80_000_000, transcendentals=0
        ),
    )(ev, data, sigma, used)


PIVOTS = 4


def inverse_factor(a):
    size = a.shape[0]
    count = size // SUBLANES
    shape = (SUBLANES, size)
    m = [a[SUBLANES * i : SUBLANES * (i + 1), :] for i in range(count)]
    diag = [None] * count
    lane = lax.broadcasted_iota(jnp.int32, shape, 1)
    sub = lax.broadcasted_iota(jnp.int32, shape, 0)

    def column(x, k):
        return jnp.broadcast_to(x[:, k : k + 1], shape)

    def row(x, r):
        return jnp.broadcast_to(x[r : r + 1, :], shape)

    for k in range(0, size, PIVOTS):
        t, r = divmod(k, SUBLANES)
        inside = (lane >= k) & (lane < k + PIVOTS)
        cols = [column(m[t], k + q) for q in range(PIVOTS)]
        pivot = {(q, p): row(cols[p], r + q) for p in range(PIVOTS) for q in range(p, PIVOTS)}
        base = [
            jnp.where(inside, jnp.where(lane == k + q, 1.0, 0.0), row(m[t], r + q))
            for q in range(PIVOTS)
        ]
        inverse = []
        for p in range(PIVOTS):
            inverse.append(1.0 / pivot[p, p])
            for q in range(p + 1, PIVOTS):
                factor = pivot[q, p] * inverse[p]
                base[q] = base[q] - factor * base[p]
                for s in range(q, PIVOTS):
                    pivot[s, q] = pivot[s, q] - factor * pivot[s, p]
        for p in range(PIVOTS):
            old = diag[t]
            diag[t] = pivot[p, p] if old is None else jnp.where(sub >= r + p, pivot[p, p], old)
        for i in range(t, count):
            cols_i = cols if i == t else [column(m[i], k + q) for q in range(PIVOTS)]
            cols_i = list(cols_i)
            if i == t:
                unit = jnp.where(lane - k == sub - r, 1.0, 0.0)
                x = jnp.where(inside & (sub >= r), unit, m[i])
            else:
                x = jnp.where(inside, 0.0, m[i])
            for p in range(PIVOTS):
                mult = cols_i[p] * inverse[p]
                if i == t:
                    mult = jnp.where(sub > r + p, mult, 0.0)
                for q in range(p + 1, PIVOTS):
                    cols_i[q] = cols_i[q] - mult * pivot[q, p]
                x = x - mult * base[p]
            m[i] = x
    out = []
    for i in range(count):
        keep = lane <= sub + SUBLANES * i
        out.append(jnp.where(keep, m[i] * lax.rsqrt(diag[i]), 0.0))
    return jnp.concatenate(out, axis=0)


def eye_mask(rows, cols):
    shape = (rows, cols)
    return lax.broadcasted_iota(jnp.int32, shape, 0) == lax.broadcasted_iota(jnp.int32, shape, 1)


def transform_kernel(g_ref, out_ref, inv_ref):
    samples = g_ref.shape[0]
    b = LANES
    ridge = float(samples - 1)
    n = samples // b
    work = {}
    for i in range(n):
        for j in range(i + 1):
            block = g_ref[i * b : (i + 1) * b, j * b : (j + 1) * b]
            work[i, j] = block + jnp.where(eye_mask(b, b), ridge, 0.0) if i == j else block
    inv = {}
    low = {}
    for k in range(n):
        inv[k, k] = inverse_factor(work[k, k])
        for i in range(k + 1, n):
            low[i, k] = dot3(work[i, k], inv[k, k], ((1,), (1,)))
        for i in range(k + 1, n):
            for j in range(k + 1, i + 1):
                work[i, j] = work[i, j] - dot3(low[i, k], low[j, k], ((1,), (1,)))
        for j in range(k):
            acc = dot3(low[k, j], inv[j, j])
            for s in range(j + 1, k):
                acc = acc + dot3(low[k, s], inv[s, j])
            inv[k, j] = -dot3(inv[k, k], acc)
    zero = jnp.zeros((b, b), jnp.float32)
    full = jnp.concatenate(
        [
            jnp.concatenate([inv[i, j] if j <= i else zero for j in range(n)], axis=1)
            for i in range(n)
        ],
        axis=0,
    )
    inv_ref[...] = full
    cross = g_ref[:, samples : samples + b]
    projected = dot3(full, cross)
    mean_weight = jnp.sum(full * projected[:, 0:1], axis=0, keepdims=True)
    out_ref[...] = math.sqrt(samples - 1) * full + mean_weight


def transform_of(gram):
    samples = gram.shape[0]
    return pl.pallas_call(
        transform_kernel,
        out_shape=jax.ShapeDtypeStruct((samples, samples), jnp.float32),
        in_specs=[VMEM_SPEC],
        out_specs=VMEM_SPEC,
        scratch_shapes=[pltpu.VMEM((samples, samples), jnp.float32)],
        cost_estimate=pl.CostEstimate(
            flops=40_000_000, bytes_accessed=40_000_000, transcendentals=0
        ),
    )(gram)


def analysis_kernel(t_ref, own_ref, side_ref, across_ref, both_ref, out_ref, x_ref):
    rank = lax.axis_index("member")
    rows = own_ref.shape[0]
    samples = x_ref.shape[0]
    side = rank + 1 - 2 * lax.rem(rank, 2)
    across = lax.rem(rank + 2, 4)
    both = lax.rem(side + 2, 4)
    pieces = ((rank, own_ref), (side, side_ref), (across, across_ref), (both, both_ref))
    total = None
    for member, ref in pieces:
        part = jnp.sum(ref[...], axis=0, keepdims=True)
        total = part if total is None else total + part
    mean = total * (1.0 / samples)
    for member, ref in pieces:
        x_ref[pl.ds(pl.multiple_of(member * rows, SUBLANES), rows), :] = ref[...] - mean
    mine = t_ref[pl.ds(pl.multiple_of(rank * rows, SUBLANES), rows), :]
    out_ref[...] = mean + dot3(mine, x_ref[...])


def analysis_chunk(transform, own, pieces, first, out, tile=1024):
    rows, points = own.shape
    samples = transform.shape[0]
    whole = pl.BlockSpec((samples, samples), lambda i: (0, 0))
    placed = pl.BlockSpec((rows, tile), lambda i: (0, i + first))
    block = pl.BlockSpec((rows, tile), lambda i: (0, i))
    kernel, extra, specs, alias = analysis_kernel, (), [], {}
    if out is not None:
        kernel = lambda t, o, s, a, b, _, *rest: analysis_kernel(t, o, s, a, b, *rest)
        extra, specs, alias = (out,), [pl.BlockSpec(memory_space=pl.ANY)], {5: 0}
    return pl.pallas_call(
        kernel,
        grid=(pieces[1].shape[1] // tile,),
        out_shape=jax.ShapeDtypeStruct((rows, points), jnp.float32),
        in_specs=[whole, placed, placed] + [block] * 2 + specs,
        out_specs=placed,
        scratch_shapes=[pltpu.VMEM((samples, tile), jnp.float32)],
        input_output_aliases=alias,
    )(transform, own, *pieces, *extra)


CHUNKS = 4


def body(prior_sample, location, data, sigma, used):
    rows, points = prior_sample.shape
    members = lax.axis_size("member")
    spaces = lax.axis_size("space")
    if members != 4 or rows % (SUBLANES * spaces) or (rows * members) % LANES:
        return general_body(prior_sample, location, data, sigma, used)
    near = [(i, i ^ 1) for i in range(members)]
    far = [(i, i ^ 2) for i in range(members)]
    width = points // CHUNKS
    parts = [prior_sample[:, i * width : (i + 1) * width] for i in range(CHUNKS)]
    across = [lax.ppermute(part, "member", far) for part in parts]
    side = lax.ppermute(prior_sample, "member", near)
    observed = gather_observed(prior_sample, location)
    gram = summed_gram(observed, data, sigma, used, members, spaces)
    *early, gram = lax.optimization_barrier((*across[:-1], gram))
    both = [lax.ppermute(part, "member", near) for part in early]
    transform = transform_of(gram)
    last, transform = lax.optimization_barrier((across[-1], transform))
    both.append(lax.ppermute(last, "member", near))
    across = (*early, last)
    out = None
    for i in range(CHUNKS):
        out = analysis_chunk(
            transform, prior_sample, (side, across[i], both[i]), i * (width // 1024), out
        )
    return out


def solution(mesh):
    placed = (
        P("member", "space"),
        P("space", None),
        P("space", None),
        P("space", None),
        P("space"),
    )
    return jax.shard_map(
        body, mesh=mesh, in_specs=placed, out_specs=P("member", "space"), check_vma=False
    )
```

```python
import functools
import math

import jax
import jax.numpy as jnp
from jax import lax
from jax.experimental import pallas as pl
from jax.experimental.pallas import tpu as pltpu
from jax.sharding import PartitionSpec as P


def solve_lower(lower_factor, target):
    return lax.linalg.triangular_solve(lower_factor, target, left_side=True, lower=True)


def general_body(
    prior_sample,
    measured_point_location,
    measured_data,
    measurement_noise_sigma,
    measured_slots_used,
):
    exact_arithmetic = lax.Precision.HIGHEST
    anomaly_matrix, points_in_region = prior_sample.shape
    region_batches = lax.axis_size("member")
    sample_total = anomaly_matrix * region_batches
    pointwise_spread = points_in_region // region_batches
    linear_position = measured_point_location.reshape(-1)
    obs_blk = linear_position.shape[0]
    observation_deviation = obs_blk // region_batches
    propagated_grid = jnp.take(prior_sample, linear_position, axis=1).reshape(
        anomaly_matrix, region_batches, observation_deviation
    )
    prior_regions = prior_sample.reshape(anomaly_matrix, region_batches, pointwise_spread)
    prior_sample_full, integrate_dynamics = (
        lax.all_to_all(prior_regions, "member", split_axis=1, concat_axis=0, tiled=True),
        lax.all_to_all(propagated_grid, "member", split_axis=1, concat_axis=0, tiled=True),
    )
    integrate_dynamics = integrate_dynamics.reshape(sample_total, observation_deviation)
    rank = lax.axis_index("member")
    start = rank * observation_deviation
    my_value = lax.dynamic_slice_in_dim(measured_data.reshape(-1), start, observation_deviation)
    my_sigma = lax.dynamic_slice_in_dim(
        measurement_noise_sigma.reshape(-1), start, observation_deviation
    )
    slots = start + jnp.arange(observation_deviation, dtype=jnp.int32)
    valid = slots < measured_slots_used[0]
    weight = jnp.where(valid, 1.0 / my_sigma, jnp.zeros_like(my_sigma))
    sim_mean = jnp.mean(integrate_dynamics, axis=0)
    perturbed = (integrate_dynamics - sim_mean[None, :]) * weight[None, :]
    innovation = (my_value - sim_mean) * weight
    gram_loc = jnp.dot(perturbed, perturbed.T, precision=exact_arithmetic)
    cross_loc = jnp.dot(perturbed, innovation, precision=exact_arithmetic)
    gram_block, cross_block = lax.psum((gram_loc, cross_loc), "member")
    gram_all, cross = lax.psum((gram_block, cross_block), "space")
    cov_matrix = gram_all + (sample_total - 1) * jnp.eye(sample_total, dtype=jnp.float32)
    lower_factor = jnp.linalg.cholesky(cov_matrix)
    inverse = solve_lower(lower_factor, jnp.eye(sample_total, dtype=jnp.float32))
    projected = jnp.dot(inverse, cross, precision=exact_arithmetic)
    mean_weight = jnp.dot(inverse.T, projected, precision=exact_arithmetic)
    weight_matrix_update = math.sqrt(sample_total - 1) * inverse + mean_weight[None, :]
    sample_vectors = prior_sample_full.reshape(sample_total, -1)
    prior_average = jnp.mean(sample_vectors, axis=0)
    updated_sample = prior_average[None, :] + jnp.dot(
        weight_matrix_update, sample_vectors - prior_average[None, :], precision=exact_arithmetic
    )
    returned = lax.all_to_all(
        updated_sample.reshape(prior_sample_full.shape),
        "member",
        split_axis=0,
        concat_axis=1,
        tiled=True,
    )
    return returned.reshape(anomaly_matrix, points_in_region)


MESH = pl.DeviceIdType.MESH
VMEM_SPEC = pl.BlockSpec(memory_space=pltpu.VMEM)
LANES = 128
MIB = 1 << 20
SUBLANES = 8


def split2(x):
    high = x.astype(jnp.bfloat16)
    low = (x - high.astype(jnp.float32)).astype(jnp.bfloat16)
    return high, low


def dot3(a, b, dims=((1,), (0,))):
    ah, al = split2(a)
    bh, bl = split2(b)
    d = functools.partial(
        lax.dot_general, dimension_numbers=(dims, ((), ())), preferred_element_type=jnp.float32
    )
    return (d(ah, bl) + d(al, bh)) + d(ah, bh)


def flat_row(ref):
    return jnp.concatenate([ref[i : i + 1, :] for i in range(ref.shape[0])], axis=1)


def gather_kernel(starts, x_ref, idx_ref, out_ref, *chunk_refs):
    step = pl.program_id(0)
    members, points = x_ref.shape
    shape = (SUBLANES, LANES)
    for (first, count), chunk_ref in zip(starts, chunk_refs):

        @pl.when((step >= first) & (step < first + count))
        def _(chunk_ref=chunk_ref):
            chunk_ref[...] = x_ref[...]

    for c in range(idx_ref.shape[0]):
        index = jnp.broadcast_to(idx_ref[c : c + 1, :], shape)
        lane = jnp.bitwise_and(index, LANES - 1)
        block = jnp.right_shift(index, LANES.bit_length() - 1) - step * (points // LANES)
        hits = [block == j for j in range(points // LANES)]
        columns = slice(c * LANES, (c + 1) * LANES)
        for g in range(0, members, SUBLANES):
            old = out_ref[g : g + SUBLANES, columns]
            got = jnp.where(step == 0, jnp.zeros(shape, jnp.float32), old)
            for j in range(points // LANES):
                x = x_ref[g : g + SUBLANES, j * LANES : (j + 1) * LANES]
                got = jnp.where(hits[j], jnp.take_along_axis(x, lane, axis=1), got)
            out_ref[g : g + SUBLANES, columns] = got


def gather_observed(prior, index, starts, tile):
    members, points = prior.shape
    slots = index.size
    f32 = jnp.float32
    return pl.pallas_call(
        functools.partial(gather_kernel, starts),
        grid=(points // tile,),
        out_shape=[jax.ShapeDtypeStruct((members, slots), f32)]
        + [jax.ShapeDtypeStruct((members, count * tile), f32) for _, count in starts],
        in_specs=[
            pl.BlockSpec((members, tile), lambda i: (0, i)),
            pl.BlockSpec(index.shape, lambda i: (0, 0)),
        ],
        out_specs=[pl.BlockSpec((members, slots), lambda i: (0, 0))]
        + [
            pl.BlockSpec(
                (members, tile),
                lambda i, first=first, count=count: (0, jnp.clip(i - first, 0, count - 1)),
            )
            for first, count in starts
        ],
        compiler_params=pltpu.CompilerParams(vmem_limit_bytes=12 * MIB),
        cost_estimate=pl.CostEstimate(
            flops=2 * members * slots * 256, bytes_accessed=16_000_000, transcendentals=0
        ),
    )(prior, index)


def send(src, dst, ssem, rsem, member, space):
    copy = pltpu.make_async_remote_copy(
        src_ref=src,
        dst_ref=dst,
        send_sem=ssem,
        recv_sem=rsem,
        device_id={"member": member, "space": space},
        device_id_type=MESH,
    )
    copy.start()
    return copy


def meet(devices):
    barrier = pltpu.get_barrier_semaphore()
    for member, space in devices:
        pl.semaphore_signal(
            barrier, inc=1, device_id={"member": member, "space": space}, device_id_type=MESH
        )
    pl.semaphore_wait(barrier, len(devices))


def neighbours():
    rank = lax.axis_index("member")
    return rank, rank + 1 - 2 * lax.rem(rank, 2), lax.rem(rank + 2, 4)


def exchange_kernel(ev_ref, out_ref, full, ssem, rsem):
    rank, side, across = neighbours()
    place = lax.axis_index("space")
    rows = ev_ref.shape[0]
    meet([(side, place), (across, place)])

    def member_rows(member):
        return full.at[pl.ds(pl.multiple_of(member * rows, SUBLANES), rows)]

    far = send(ev_ref, member_rows(rank), ssem.at[0], rsem.at[0], across, place)
    near = send(ev_ref, member_rows(rank), ssem.at[1], rsem.at[1], side, place)
    far.wait_recv()
    got = member_rows(across)
    relay = send(got, got, ssem.at[2], rsem.at[2], side, place)
    near.wait_recv()
    relay.wait_recv()
    full[pl.ds(pl.multiple_of(rank * rows, SUBLANES), rows), :] = ev_ref[...]
    for copy in (far, near, relay):
        copy.wait_send()
    out_ref[...] = full[...]


def exchange_observed(ev, members):
    rows, slots = ev.shape
    dma = pltpu.SemaphoreType.DMA
    full = (rows * members, slots)
    return pl.pallas_call(
        exchange_kernel,
        out_shape=jax.ShapeDtypeStruct(full, jnp.float32),
        in_specs=[VMEM_SPEC],
        out_specs=VMEM_SPEC,
        scratch_shapes=[pltpu.VMEM(full, jnp.float32), dma((3,)), dma((3,))],
        compiler_params=pltpu.CompilerParams(collective_id=0, has_side_effects=True, vmem_limit_bytes=4 * MIB),
        cost_estimate=pl.CostEstimate(
            flops=1_000_000, bytes_accessed=30_000_000, transcendentals=0
        ),
    )(ev)


def gram_kernel(
    spaces,
    ev_ref,
    data_ref,
    sigma_ref,
    used_ref,
    out_ref,
    gram,
    parts,
    total,
    rs_send,
    rs_recv,
    ag_send,
    ag_recv,
    fin_send,
    fin_recv,
):
    rank, side, _ = neighbours()
    place = lax.axis_index("space")
    half = lax.rem(rank, 2)
    samples, slots = ev_ref.shape
    rows = samples // 2
    chunk = rows // spaces
    meet([(side, place)] + [(rank, lax.rem(place + d, spaces)) for d in range(1, spaces)])

    slot = lax.broadcasted_iota(jnp.int32, (1, slots), 1)
    weight = jnp.where(slot < used_ref[0], 1.0 / flat_row(sigma_ref), 0.0)
    ev = ev_ref[...]
    mean = jnp.sum(ev, axis=0, keepdims=True) * (1.0 / samples)
    anomalies = (ev - mean) * weight
    innovation = (flat_row(data_ref) - mean) * weight
    first = lax.broadcasted_iota(jnp.int32, (LANES, slots), 0) == 0
    extra = jnp.where(first, jnp.broadcast_to(innovation, (LANES, slots)), 0.0)
    mine = (ev_ref[pl.ds(pl.multiple_of(half * rows, SUBLANES), rows), :] - mean) * weight
    right = jnp.concatenate([anomalies, extra], axis=0)
    gram[...] = dot3(mine, right, ((1,), (1,)))

    copies = []
    for d in range(1, spaces):
        other = lax.rem(place + d, spaces)
        copies.append(
            send(
                gram.at[pl.ds(pl.multiple_of(other * chunk, SUBLANES), chunk)],
                parts.at[d - 1],
                rs_send.at[d - 1],
                rs_recv.at[d - 1],
                rank,
                other,
            )
        )
    acc = gram[pl.ds(pl.multiple_of(place * chunk, SUBLANES), chunk), :]
    for d in range(1, spaces):
        copies[d - 1].wait_recv()
        acc = acc + parts[d - 1]
    piece = pl.ds(pl.multiple_of(half * rows + place * chunk, SUBLANES), chunk)
    total[piece, :] = acc
    spread = []
    for d in range(1, spaces):
        other = lax.rem(place + d, spaces)
        spread.append(
            send(
                total.at[piece], total.at[piece], ag_send.at[d - 1], ag_recv.at[d - 1], rank, other
            )
        )
    for copy in spread:
        copy.wait_recv()
    mine_rows = total.at[pl.ds(pl.multiple_of(half * rows, SUBLANES), rows)]
    last = send(mine_rows, mine_rows, fin_send, fin_recv, side, place)
    last.wait_recv()
    for copy in (*copies, *spread, last):
        copy.wait_send()
    out_ref[...] = total[...]


def summed_gram(ev, data, sigma, used, spaces):
    samples, _ = ev.shape
    rows = samples // 2
    width = samples + LANES
    dma = pltpu.SemaphoreType.DMA
    return pl.pallas_call(
        functools.partial(gram_kernel, spaces),
        out_shape=jax.ShapeDtypeStruct((samples, width), jnp.float32),
        in_specs=[VMEM_SPEC] * 3 + [pl.BlockSpec(memory_space=pltpu.SMEM)],
        out_specs=VMEM_SPEC,
        scratch_shapes=[
            pltpu.VMEM((rows, width), jnp.float32),
            pltpu.VMEM((spaces - 1, rows // spaces, width), jnp.float32),
            pltpu.VMEM((samples, width), jnp.float32),
            dma((spaces - 1,)),
            dma((spaces - 1,)),
            dma((spaces - 1,)),
            dma((spaces - 1,)),
            dma(()),
            dma(()),
        ],
        compiler_params=pltpu.CompilerParams(collective_id=1, has_side_effects=True, vmem_limit_bytes=16 * MIB),
        cost_estimate=pl.CostEstimate(
            flops=4_000_000, bytes_accessed=6_000_000, transcendentals=0
        ),
    )(ev, data, sigma, used)


PIVOTS = 4


def inverse_factor(a):
    size = a.shape[0]
    count = size // SUBLANES
    shape = (SUBLANES, size)
    m = [a[SUBLANES * i : SUBLANES * (i + 1), :] for i in range(count)]
    diag = [None] * count
    lane = lax.broadcasted_iota(jnp.int32, shape, 1)
    sub = lax.broadcasted_iota(jnp.int32, shape, 0)

    def column(x, k):
        return jnp.broadcast_to(x[:, k : k + 1], shape)

    def row(x, r):
        return jnp.broadcast_to(x[r : r + 1, :], shape)

    for k in range(0, size, PIVOTS):
        t, r = divmod(k, SUBLANES)
        inside = (lane >= k) & (lane < k + PIVOTS)
        cols = [column(m[t], k + q) for q in range(PIVOTS)]
        pivot = {(q, p): row(cols[p], r + q) for p in range(PIVOTS) for q in range(p, PIVOTS)}
        base = [
            jnp.where(inside, jnp.where(lane == k + q, 1.0, 0.0), row(m[t], r + q))
            for q in range(PIVOTS)
        ]
        inverse = []
        for p in range(PIVOTS):
            inverse.append(1.0 / pivot[p, p])
            for q in range(p + 1, PIVOTS):
                factor = pivot[q, p] * inverse[p]
                base[q] = base[q] - factor * base[p]
                for s in range(q, PIVOTS):
                    pivot[s, q] = pivot[s, q] - factor * pivot[s, p]
        for p in range(PIVOTS):
            old = diag[t]
            diag[t] = pivot[p, p] if old is None else jnp.where(sub >= r + p, pivot[p, p], old)
        for i in range(t, count):
            cols_i = cols if i == t else [column(m[i], k + q) for q in range(PIVOTS)]
            cols_i = list(cols_i)
            if i == t:
                unit = jnp.where(lane - k == sub - r, 1.0, 0.0)
                x = jnp.where(inside & (sub >= r), unit, m[i])
            else:
                x = jnp.where(inside, 0.0, m[i])
            for p in range(PIVOTS):
                mult = cols_i[p] * inverse[p]
                if i == t:
                    mult = jnp.where(sub > r + p, mult, 0.0)
                for q in range(p + 1, PIVOTS):
                    cols_i[q] = cols_i[q] - mult * pivot[q, p]
                x = x - mult * base[p]
            m[i] = x
    out = []
    for i in range(count):
        keep = lane <= sub + SUBLANES * i
        out.append(jnp.where(keep, m[i] * lax.rsqrt(diag[i]), 0.0))
    return jnp.concatenate(out, axis=0)


def eye_mask(rows, cols):
    shape = (rows, cols)
    return lax.broadcasted_iota(jnp.int32, shape, 0) == lax.broadcasted_iota(jnp.int32, shape, 1)


def transform_kernel(g_ref, out_ref, inv_ref):
    samples = g_ref.shape[0]
    b = LANES
    ridge = float(samples - 1)
    n = samples // b
    work = {}
    for i in range(n):
        for j in range(i + 1):
            block = g_ref[i * b : (i + 1) * b, j * b : (j + 1) * b]
            work[i, j] = block + jnp.where(eye_mask(b, b), ridge, 0.0) if i == j else block
    inv = {}
    low = {}
    for k in range(n):
        inv[k, k] = inverse_factor(work[k, k])
        for i in range(k + 1, n):
            low[i, k] = dot3(work[i, k], inv[k, k], ((1,), (1,)))
        for i in range(k + 1, n):
            for j in range(k + 1, i + 1):
                work[i, j] = work[i, j] - dot3(low[i, k], low[j, k], ((1,), (1,)))
        for j in range(k):
            acc = dot3(low[k, j], inv[j, j])
            for s in range(j + 1, k):
                acc = acc + dot3(low[k, s], inv[s, j])
            inv[k, j] = -dot3(inv[k, k], acc)
    zero = jnp.zeros((b, b), jnp.float32)
    full = jnp.concatenate(
        [
            jnp.concatenate([inv[i, j] if j <= i else zero for j in range(n)], axis=1)
            for i in range(n)
        ],
        axis=0,
    )
    inv_ref[...] = full
    cross = g_ref[:, samples : samples + b]
    projected = dot3(full, cross)
    mean_weight = jnp.sum(full * projected[:, 0:1], axis=0, keepdims=True)
    out_ref[...] = math.sqrt(samples - 1) * full + mean_weight


def transform_of(gram):
    samples = gram.shape[0]
    return pl.pallas_call(
        transform_kernel,
        out_shape=jax.ShapeDtypeStruct((samples, samples), jnp.float32),
        in_specs=[VMEM_SPEC],
        out_specs=VMEM_SPEC,
        scratch_shapes=[pltpu.VMEM((samples, samples), jnp.float32)],
        compiler_params=pltpu.CompilerParams(vmem_limit_bytes=8 * MIB),
        cost_estimate=pl.CostEstimate(
            flops=4_000_000, bytes_accessed=4_000_000, transcendentals=0
        ),
    )(gram)


def analysis_kernel(t_ref, own_ref, side_ref, across_ref, both_ref, out_ref, x_ref):
    rank = lax.axis_index("member")
    rows = own_ref.shape[0]
    samples = x_ref.shape[0]
    side = rank + 1 - 2 * lax.rem(rank, 2)
    across = lax.rem(rank + 2, 4)
    both = lax.rem(side + 2, 4)
    pieces = ((rank, own_ref), (side, side_ref), (across, across_ref), (both, both_ref))
    total = None
    for member, ref in pieces:
        part = jnp.sum(ref[...], axis=0, keepdims=True)
        total = part if total is None else total + part
    mean = total * (1.0 / samples)
    for member, ref in pieces:
        x_ref[pl.ds(pl.multiple_of(member * rows, SUBLANES), rows), :] = ref[...] - mean
    mine = t_ref[pl.ds(pl.multiple_of(rank * rows, SUBLANES), rows), :]
    th, tl = split2(mine)
    xh, xl = split2(x_ref[...])
    dot = functools.partial(jnp.dot, preferred_element_type=jnp.float32)
    both_parts = dot(jnp.concatenate([th, tl], axis=0), xh)
    out_ref[...] = mean + ((both_parts[rows:] + dot(th, xl)) + both_parts[:rows])


def analysis_chunk(transform, own, pieces, first, out, tile=1024):
    rows, points = own.shape
    samples = transform.shape[0]
    whole = pl.BlockSpec((samples, samples), lambda i: (0, 0))
    placed = pl.BlockSpec((rows, tile), lambda i: (0, i + first))
    block = pl.BlockSpec((rows, tile), lambda i: (0, i))
    kernel, extra, specs, alias = analysis_kernel, (), [], {}
    if out is not None:
        kernel = lambda t, o, s, a, b, _, *rest: analysis_kernel(t, o, s, a, b, *rest)
        extra, specs, alias = (out,), [pl.BlockSpec(memory_space=pl.ANY)], {5: 0}
    return pl.pallas_call(
        kernel,
        grid=(pieces[1].shape[1] // tile,),
        out_shape=jax.ShapeDtypeStruct((rows, points), jnp.float32),
        in_specs=[whole, placed, placed] + [block] * 2 + specs,
        out_specs=placed,
        scratch_shapes=[pltpu.VMEM((samples, tile), jnp.float32)],
        input_output_aliases=alias,
        compiler_params=pltpu.CompilerParams(vmem_limit_bytes=12 * MIB),
    )(transform, own, *pieces, *extra)


TILE = 1024
EIGHTHS = (2, 2, 2, 2)


def body(*arrays):
    prior_sample = arrays[0]
    rows, points = prior_sample.shape
    members, spaces = lax.axis_size("member"), lax.axis_size("space")
    if (
        members != 4
        or rows * members % (2 * SUBLANES * spaces)
        or rows * members % LANES
        or rows % SUBLANES
        or points % (8 * TILE)
    ):
        return general_body(*arrays)
    return fast_body(members, spaces, *arrays)


def fast_body(members, spaces, prior_sample, location, data, sigma, used):
    points = prior_sample.shape[1]
    near = [(i, i ^ 1) for i in range(members)]
    far = [(i, i ^ 2) for i in range(members)]
    counts = [e * points // (8 * TILE) for e in EIGHTHS]
    starts = [(sum(counts[:i]), n) for i, n in enumerate(counts)]
    across = [lax.ppermute(prior_sample[:, : counts[0] * TILE], "member", far)]
    side = lax.ppermute(prior_sample, "member", near)
    observed, *chunks = gather_observed(prior_sample, location, starts[1:], TILE)
    gathered = exchange_observed(observed, members)
    *chunks, gathered = lax.optimization_barrier((*chunks, gathered))
    for chunk in chunks:
        across.append(lax.ppermute(chunk, "member", far))
    gram = summed_gram(gathered, data, sigma, used, spaces)
    across[0], gram = lax.optimization_barrier((across[0], gram))
    both = lax.ppermute(across[0], "member", near)
    out = transform = transform_of(gram)
    result = None
    for i, (first, _) in enumerate(starts):
        now = both
        if i + 1 < len(starts):
            across[i + 1], out = lax.optimization_barrier((across[i + 1], out))
            if i == 0:
                transform = out
            else:
                result = out
            both = lax.ppermute(across[i + 1], "member", near)
        result = analysis_chunk(
            transform, prior_sample, (side, across[i], now), first, result
        )
        out = result
    return result


def solution(mesh):
    placed = (
        P("member", "space"),
        P("space", None),
        P("space", None),
        P("space", None),
        P("space"),
    )
    return jax.shard_map(
        body, mesh=mesh, in_specs=placed, out_specs=P("member", "space"), check_vma=False
    )
```

```python
import functools
import math

import jax
import jax.numpy as jnp
from jax import lax
from jax.experimental import pallas as pl
from jax.experimental.pallas import tpu as pltpu
from jax.sharding import PartitionSpec as P


def solve_lower(lower_factor, target):
    return lax.linalg.triangular_solve(lower_factor, target, left_side=True, lower=True)


def general_body(
    prior_sample,
    measured_point_location,
    measured_data,
    measurement_noise_sigma,
    measured_slots_used,
):
    exact_arithmetic = lax.Precision.HIGHEST
    anomaly_matrix, points_in_region = prior_sample.shape
    region_batches = lax.axis_size("member")
    sample_total = anomaly_matrix * region_batches
    pointwise_spread = points_in_region // region_batches
    linear_position = measured_point_location.reshape(-1)
    obs_blk = linear_position.shape[0]
    observation_deviation = obs_blk // region_batches
    propagated_grid = jnp.take(prior_sample, linear_position, axis=1).reshape(
        anomaly_matrix, region_batches, observation_deviation
    )
    prior_regions = prior_sample.reshape(anomaly_matrix, region_batches, pointwise_spread)
    prior_sample_full, integrate_dynamics = (
        lax.all_to_all(prior_regions, "member", split_axis=1, concat_axis=0, tiled=True),
        lax.all_to_all(propagated_grid, "member", split_axis=1, concat_axis=0, tiled=True),
    )
    integrate_dynamics = integrate_dynamics.reshape(sample_total, observation_deviation)
    rank = lax.axis_index("member")
    start = rank * observation_deviation
    my_value = lax.dynamic_slice_in_dim(measured_data.reshape(-1), start, observation_deviation)
    my_sigma = lax.dynamic_slice_in_dim(
        measurement_noise_sigma.reshape(-1), start, observation_deviation
    )
    slots = start + jnp.arange(observation_deviation, dtype=jnp.int32)
    valid = slots < measured_slots_used[0]
    weight = jnp.where(valid, 1.0 / my_sigma, jnp.zeros_like(my_sigma))
    sim_mean = jnp.mean(integrate_dynamics, axis=0)
    perturbed = (integrate_dynamics - sim_mean[None, :]) * weight[None, :]
    innovation = (my_value - sim_mean) * weight
    gram_loc = jnp.dot(perturbed, perturbed.T, precision=exact_arithmetic)
    cross_loc = jnp.dot(perturbed, innovation, precision=exact_arithmetic)
    gram_block, cross_block = lax.psum((gram_loc, cross_loc), "member")
    gram_all, cross = lax.psum((gram_block, cross_block), "space")
    cov_matrix = gram_all + (sample_total - 1) * jnp.eye(sample_total, dtype=jnp.float32)
    lower_factor = jnp.linalg.cholesky(cov_matrix)
    inverse = solve_lower(lower_factor, jnp.eye(sample_total, dtype=jnp.float32))
    projected = jnp.dot(inverse, cross, precision=exact_arithmetic)
    mean_weight = jnp.dot(inverse.T, projected, precision=exact_arithmetic)
    weight_matrix_update = math.sqrt(sample_total - 1) * inverse + mean_weight[None, :]
    sample_vectors = prior_sample_full.reshape(sample_total, -1)
    prior_average = jnp.mean(sample_vectors, axis=0)
    updated_sample = prior_average[None, :] + jnp.dot(
        weight_matrix_update, sample_vectors - prior_average[None, :], precision=exact_arithmetic
    )
    returned = lax.all_to_all(
        updated_sample.reshape(prior_sample_full.shape),
        "member",
        split_axis=0,
        concat_axis=1,
        tiled=True,
    )
    return returned.reshape(anomaly_matrix, points_in_region)


MESH = pl.DeviceIdType.MESH
VMEM_SPEC = pl.BlockSpec(memory_space=pltpu.VMEM)
LANES = 128
MIB = 1 << 20
SUBLANES = 8


def split2(x):
    high = x.astype(jnp.bfloat16)
    low = (x - high.astype(jnp.float32)).astype(jnp.bfloat16)
    return high, low


def dot3(a, b, dims=((1,), (0,))):
    ah, al = split2(a)
    bh, bl = split2(b)
    d = functools.partial(
        lax.dot_general, dimension_numbers=(dims, ((), ())), preferred_element_type=jnp.float32
    )
    return (d(ah, bl) + d(al, bh)) + d(ah, bh)


def flat_row(ref):
    return jnp.concatenate([ref[i : i + 1, :] for i in range(ref.shape[0])], axis=1)


def gather_kernel(starts, x_ref, idx_ref, out_ref, *chunk_refs):
    step = pl.program_id(0)
    members, points = x_ref.shape
    shape = (SUBLANES, LANES)
    for (first, count), chunk_ref in zip(starts, chunk_refs):

        @pl.when((step >= first) & (step < first + count))
        def _(chunk_ref=chunk_ref):
            chunk_ref[...] = x_ref[...]

    for c in range(idx_ref.shape[0]):
        index = jnp.broadcast_to(idx_ref[c : c + 1, :], shape)
        lane = jnp.bitwise_and(index, LANES - 1)
        block = jnp.right_shift(index, LANES.bit_length() - 1) - step * (points // LANES)
        hits = [block == j for j in range(points // LANES)]
        columns = slice(c * LANES, (c + 1) * LANES)
        for g in range(0, members, SUBLANES):
            old = out_ref[g : g + SUBLANES, columns]
            got = jnp.where(step == 0, jnp.zeros(shape, jnp.float32), old)
            for j in range(points // LANES):
                x = x_ref[g : g + SUBLANES, j * LANES : (j + 1) * LANES]
                got = jnp.where(hits[j], jnp.take_along_axis(x, lane, axis=1), got)
            out_ref[g : g + SUBLANES, columns] = got


def gather_observed(prior, index, starts, tile):
    members, points = prior.shape
    slots = index.size
    f32 = jnp.float32
    return pl.pallas_call(
        functools.partial(gather_kernel, starts),
        grid=(points // tile,),
        out_shape=[jax.ShapeDtypeStruct((members, slots), f32)]
        + [jax.ShapeDtypeStruct((members, count * tile), f32) for _, count in starts],
        in_specs=[
            pl.BlockSpec((members, tile), lambda i: (0, i)),
            pl.BlockSpec(index.shape, lambda i: (0, 0)),
        ],
        out_specs=[pl.BlockSpec((members, slots), lambda i: (0, 0))]
        + [
            pl.BlockSpec(
                (members, tile),
                lambda i, first=first, count=count: (0, jnp.clip(i - first, 0, count - 1)),
            )
            for first, count in starts
        ],
        compiler_params=pltpu.CompilerParams(vmem_limit_bytes=12 * MIB),
        cost_estimate=pl.CostEstimate(
            flops=2 * members * slots * 256, bytes_accessed=16_000_000, transcendentals=0
        ),
    )(prior, index)


def send(src, dst, ssem, rsem, member, space):
    copy = pltpu.make_async_remote_copy(
        src_ref=src,
        dst_ref=dst,
        send_sem=ssem,
        recv_sem=rsem,
        device_id={"member": member, "space": space},
        device_id_type=MESH,
    )
    copy.start()
    return copy


def meet(devices):
    barrier = pltpu.get_barrier_semaphore()
    for member, space in devices:
        pl.semaphore_signal(
            barrier, inc=1, device_id={"member": member, "space": space}, device_id_type=MESH
        )
    pl.semaphore_wait(barrier, len(devices))


def neighbours():
    rank = lax.axis_index("member")
    return rank, rank + 1 - 2 * lax.rem(rank, 2), lax.rem(rank + 2, 4)


def exchange_kernel(ev_ref, out_ref, pair, ssem, rsem):
    rank, _, across = neighbours()
    place = lax.axis_index("space")
    rows = ev_ref.shape[0]
    meet([(across, place)])
    mine = pl.ds(pl.multiple_of((rank // 2) * rows, SUBLANES), rows)
    copy = send(ev_ref, pair.at[mine], ssem, rsem, across, place)
    pair[mine, :] = ev_ref[...]
    copy.wait()
    out_ref[...] = pair[...]


def exchange_observed(ev):
    rows, slots = ev.shape
    dma = pltpu.SemaphoreType.DMA
    pair = (rows * 2, slots)
    return pl.pallas_call(
        exchange_kernel,
        out_shape=jax.ShapeDtypeStruct(pair, jnp.float32),
        in_specs=[VMEM_SPEC],
        out_specs=VMEM_SPEC,
        scratch_shapes=[pltpu.VMEM(pair, jnp.float32), dma(()), dma(())],
        compiler_params=pltpu.CompilerParams(
            collective_id=0, has_side_effects=True, vmem_limit_bytes=4 * MIB
        ),
        cost_estimate=pl.CostEstimate(
            flops=1_000_000, bytes_accessed=20_000_000, transcendentals=0
        ),
    )(ev)


def gram_kernel(
    spaces,
    ev_ref,
    data_ref,
    sigma_ref,
    used_ref,
    out_ref,
    full,
    gram,
    parts,
    total,
    rs_send,
    rs_recv,
    ag_send,
    ag_recv,
    fin_send,
    fin_recv,
    ex_send,
    ex_recv,
):
    rank, side, _ = neighbours()
    place = lax.axis_index("space")
    half = lax.rem(rank, 2)
    samples, slots = full.shape
    rows = samples // 2
    group = samples // 4
    chunk = rows // spaces
    meet([(side, place)] + [(rank, lax.rem(place + d, spaces)) for d in range(1, spaces)])

    shared = []
    for i in range(2):
        source = ev_ref.at[pl.ds(i * group, group)]
        target = full.at[pl.ds(pl.multiple_of((half + 2 * i) * group, SUBLANES), group)]
        shared.append(send(source, target, ex_send.at[i], ex_recv.at[i], side, place))
    for i in range(2):
        own = pl.ds(pl.multiple_of((half + 2 * i) * group, SUBLANES), group)
        full[own, :] = ev_ref[i * group : (i + 1) * group, :]
    slot = lax.broadcasted_iota(jnp.int32, (1, slots), 1)
    weight = jnp.where(slot < used_ref[0], 1.0 / flat_row(sigma_ref), 0.0)
    for copy in shared:
        copy.wait_recv()
    ev = full[...]
    mean = jnp.sum(ev, axis=0, keepdims=True) * (1.0 / samples)
    anomalies = (ev - mean) * weight
    innovation = (flat_row(data_ref) - mean) * weight
    first = lax.broadcasted_iota(jnp.int32, (LANES, slots), 0) == 0
    extra = jnp.where(first, jnp.broadcast_to(innovation, (LANES, slots)), 0.0)
    mine = (full[pl.ds(pl.multiple_of(half * rows, SUBLANES), rows), :] - mean) * weight
    right = jnp.concatenate([anomalies, extra], axis=0)
    gram[...] = dot3(mine, right, ((1,), (1,)))

    copies = []
    for d in range(1, spaces):
        other = lax.rem(place + d, spaces)
        copies.append(
            send(
                gram.at[pl.ds(pl.multiple_of(other * chunk, SUBLANES), chunk)],
                parts.at[d - 1],
                rs_send.at[d - 1],
                rs_recv.at[d - 1],
                rank,
                other,
            )
        )
    acc = gram[pl.ds(pl.multiple_of(place * chunk, SUBLANES), chunk), :]
    for d in range(1, spaces):
        copies[d - 1].wait_recv()
        acc = acc + parts[d - 1]
    piece = pl.ds(pl.multiple_of(half * rows + place * chunk, SUBLANES), chunk)
    total[piece, :] = acc
    spread = []
    for d in range(1, spaces):
        other = lax.rem(place + d, spaces)
        spread.append(
            send(
                total.at[piece], total.at[piece], ag_send.at[d - 1], ag_recv.at[d - 1], rank, other
            )
        )
    for copy in spread:
        copy.wait_recv()
    mine_rows = total.at[pl.ds(pl.multiple_of(half * rows, SUBLANES), rows)]
    last = send(mine_rows, mine_rows, fin_send, fin_recv, side, place)
    last.wait_recv()
    for copy in (*shared, *copies, *spread, last):
        copy.wait_send()
    out_ref[...] = total[...]


def summed_gram(ev, data, sigma, used, spaces):
    rows, slots = ev.shape
    samples = rows * 2
    width = samples + LANES
    dma = pltpu.SemaphoreType.DMA
    return pl.pallas_call(
        functools.partial(gram_kernel, spaces),
        out_shape=jax.ShapeDtypeStruct((samples, width), jnp.float32),
        in_specs=[VMEM_SPEC] * 3 + [pl.BlockSpec(memory_space=pltpu.SMEM)],
        out_specs=VMEM_SPEC,
        scratch_shapes=[
            pltpu.VMEM((samples, slots), jnp.float32),
            pltpu.VMEM((rows, width), jnp.float32),
            pltpu.VMEM((spaces - 1, rows // spaces, width), jnp.float32),
            pltpu.VMEM((samples, width), jnp.float32),
            dma((spaces - 1,)),
            dma((spaces - 1,)),
            dma((spaces - 1,)),
            dma((spaces - 1,)),
            dma(()),
            dma(()),
            dma((2,)),
            dma((2,)),
        ],
        compiler_params=pltpu.CompilerParams(collective_id=1, has_side_effects=True, vmem_limit_bytes=16 * MIB),
        cost_estimate=pl.CostEstimate(
            flops=4_000_000, bytes_accessed=6_000_000, transcendentals=0
        ),
    )(ev, data, sigma, used)


PIVOTS = 4


def inverse_factor(a):
    size = a.shape[0]
    count = size // SUBLANES
    shape = (SUBLANES, size)
    m = [a[SUBLANES * i : SUBLANES * (i + 1), :] for i in range(count)]
    diag = [None] * count
    lane = lax.broadcasted_iota(jnp.int32, shape, 1)
    sub = lax.broadcasted_iota(jnp.int32, shape, 0)

    def column(x, k):
        return jnp.broadcast_to(x[:, k : k + 1], shape)

    def row(x, r):
        return jnp.broadcast_to(x[r : r + 1, :], shape)

    for k in range(0, size, PIVOTS):
        t, r = divmod(k, SUBLANES)
        inside = (lane >= k) & (lane < k + PIVOTS)
        cols = [column(m[t], k + q) for q in range(PIVOTS)]
        pivot = {(q, p): row(cols[p], r + q) for p in range(PIVOTS) for q in range(p, PIVOTS)}
        base = [
            jnp.where(inside, jnp.where(lane == k + q, 1.0, 0.0), row(m[t], r + q))
            for q in range(PIVOTS)
        ]
        inverse = []
        for p in range(PIVOTS):
            inverse.append(1.0 / pivot[p, p])
            for q in range(p + 1, PIVOTS):
                factor = pivot[q, p] * inverse[p]
                base[q] = base[q] - factor * base[p]
                for s in range(q, PIVOTS):
                    pivot[s, q] = pivot[s, q] - factor * pivot[s, p]
        for p in range(PIVOTS):
            old = diag[t]
            diag[t] = pivot[p, p] if old is None else jnp.where(sub >= r + p, pivot[p, p], old)
        for i in range(t, count):
            cols_i = cols if i == t else [column(m[i], k + q) for q in range(PIVOTS)]
            cols_i = list(cols_i)
            if i == t:
                unit = jnp.where(lane - k == sub - r, 1.0, 0.0)
                x = jnp.where(inside & (sub >= r), unit, m[i])
            else:
                x = jnp.where(inside, 0.0, m[i])
            for p in range(PIVOTS):
                mult = cols_i[p] * inverse[p]
                if i == t:
                    mult = jnp.where(sub > r + p, mult, 0.0)
                for q in range(p + 1, PIVOTS):
                    cols_i[q] = cols_i[q] - mult * pivot[q, p]
                x = x - mult * base[p]
            m[i] = x
    out = []
    for i in range(count):
        keep = lane <= sub + SUBLANES * i
        out.append(jnp.where(keep, m[i] * lax.rsqrt(diag[i]), 0.0))
    return jnp.concatenate(out, axis=0)


def eye_mask(rows, cols):
    shape = (rows, cols)
    return lax.broadcasted_iota(jnp.int32, shape, 0) == lax.broadcasted_iota(jnp.int32, shape, 1)


def transform_kernel(g_ref, out_ref, inv_ref):
    samples = g_ref.shape[0]
    b = LANES
    ridge = float(samples - 1)
    n = samples // b
    work = {}
    for i in range(n):
        for j in range(i + 1):
            block = g_ref[i * b : (i + 1) * b, j * b : (j + 1) * b]
            work[i, j] = block + jnp.where(eye_mask(b, b), ridge, 0.0) if i == j else block
    inv = {}
    low = {}
    for k in range(n):
        inv[k, k] = inverse_factor(work[k, k])
        for i in range(k + 1, n):
            low[i, k] = dot3(work[i, k], inv[k, k], ((1,), (1,)))
        for i in range(k + 1, n):
            for j in range(k + 1, i + 1):
                work[i, j] = work[i, j] - dot3(low[i, k], low[j, k], ((1,), (1,)))
        for j in range(k):
            acc = dot3(low[k, j], inv[j, j])
            for s in range(j + 1, k):
                acc = acc + dot3(low[k, s], inv[s, j])
            inv[k, j] = -dot3(inv[k, k], acc)
    zero = jnp.zeros((b, b), jnp.float32)
    full = jnp.concatenate(
        [
            jnp.concatenate([inv[i, j] if j <= i else zero for j in range(n)], axis=1)
            for i in range(n)
        ],
        axis=0,
    )
    inv_ref[...] = full
    cross = g_ref[:, samples : samples + b]
    projected = dot3(full, cross)
    mean_weight = jnp.sum(full * projected[:, 0:1], axis=0, keepdims=True)
    out_ref[...] = math.sqrt(samples - 1) * full + mean_weight


def transform_of(gram):
    samples = gram.shape[0]
    return pl.pallas_call(
        transform_kernel,
        out_shape=jax.ShapeDtypeStruct((samples, samples), jnp.float32),
        in_specs=[VMEM_SPEC],
        out_specs=VMEM_SPEC,
        scratch_shapes=[pltpu.VMEM((samples, samples), jnp.float32)],
        compiler_params=pltpu.CompilerParams(vmem_limit_bytes=8 * MIB),
        cost_estimate=pl.CostEstimate(
            flops=4_000_000, bytes_accessed=4_000_000, transcendentals=0
        ),
    )(gram)


def analysis_kernel(t_ref, own_ref, side_ref, across_ref, both_ref, out_ref, x_ref):
    rank = lax.axis_index("member")
    rows = own_ref.shape[0]
    samples = x_ref.shape[0]
    side = rank + 1 - 2 * lax.rem(rank, 2)
    across = lax.rem(rank + 2, 4)
    both = lax.rem(side + 2, 4)
    pieces = ((rank, own_ref), (side, side_ref), (across, across_ref), (both, both_ref))
    total = None
    for member, ref in pieces:
        part = jnp.sum(ref[...], axis=0, keepdims=True)
        total = part if total is None else total + part
    mean = total * (1.0 / samples)
    for member, ref in pieces:
        x_ref[pl.ds(pl.multiple_of(member * rows, SUBLANES), rows), :] = ref[...] - mean
    mine = t_ref[pl.ds(pl.multiple_of(rank * rows, SUBLANES), rows), :]
    th, tl = split2(mine)
    xh, xl = split2(x_ref[...])
    dot = functools.partial(jnp.dot, preferred_element_type=jnp.float32)
    both_parts = dot(jnp.concatenate([th, tl], axis=0), xh)
    out_ref[...] = mean + ((both_parts[rows:] + dot(th, xl)) + both_parts[:rows])


def analysis_chunk(transform, own, pieces, first, out, tile=1024):
    rows, points = own.shape
    samples = transform.shape[0]
    whole = pl.BlockSpec((samples, samples), lambda i: (0, 0))
    placed = pl.BlockSpec((rows, tile), lambda i: (0, i + first))
    block = pl.BlockSpec((rows, tile), lambda i: (0, i))
    kernel, extra, specs, alias = analysis_kernel, (), [], {}
    if out is not None:
        kernel = lambda t, o, s, a, b, _, *rest: analysis_kernel(t, o, s, a, b, *rest)
        extra, specs, alias = (out,), [pl.BlockSpec(memory_space=pl.ANY)], {5: 0}
    return pl.pallas_call(
        kernel,
        grid=(pieces[1].shape[1] // tile,),
        out_shape=jax.ShapeDtypeStruct((rows, points), jnp.float32),
        in_specs=[whole, placed, placed] + [block] * 2 + specs,
        out_specs=placed,
        scratch_shapes=[pltpu.VMEM((samples, tile), jnp.float32)],
        input_output_aliases=alias,
        compiler_params=pltpu.CompilerParams(vmem_limit_bytes=12 * MIB),
    )(transform, own, *pieces, *extra)


TILE = 1024
EIGHTHS = (1, 3, 3, 1)


def body(*arrays):
    prior_sample = arrays[0]
    rows, points = prior_sample.shape
    members, spaces = lax.axis_size("member"), lax.axis_size("space")
    if (
        members != 4
        or rows * members % (2 * SUBLANES * spaces)
        or rows * members % LANES
        or rows % SUBLANES
        or points % (8 * TILE)
    ):
        return general_body(*arrays)
    return fast_body(members, spaces, *arrays)


def fast_body(members, spaces, prior_sample, location, data, sigma, used):
    points = prior_sample.shape[1]
    near = [(i, i ^ 1) for i in range(members)]
    far = [(i, i ^ 2) for i in range(members)]
    counts = [e * points // (8 * TILE) for e in EIGHTHS]
    starts = [(sum(counts[:i]), n) for i, n in enumerate(counts)]
    across = [lax.ppermute(prior_sample[:, : counts[0] * TILE], "member", far)]
    side = lax.ppermute(prior_sample, "member", near)
    observed, *chunks = gather_observed(prior_sample, location, starts[1:], TILE)
    gathered = exchange_observed(observed)
    *chunks, gathered = lax.optimization_barrier((*chunks, gathered))
    for chunk in chunks:
        across.append(lax.ppermute(chunk, "member", far))
    gram = summed_gram(gathered, data, sigma, used, spaces)
    across[0], gram = lax.optimization_barrier((across[0], gram))
    both = lax.ppermute(across[0], "member", near)
    out = transform = transform_of(gram)
    result = None
    for i, (first, _) in enumerate(starts):
        now = both
        if i + 1 < len(starts):
            across[i + 1], out = lax.optimization_barrier((across[i + 1], out))
            if i == 0:
                transform = out
            else:
                result = out
            both = lax.ppermute(across[i + 1], "member", near)
        result = analysis_chunk(
            transform, prior_sample, (side, across[i], now), first, result
        )
        out = result
    return result


def solution(mesh):
    placed = (
        P("member", "space"),
        P("space", None),
        P("space", None),
        P("space", None),
        P("space"),
    )
    return jax.shard_map(
        body, mesh=mesh, in_specs=placed, out_specs=P("member", "space"), check_vma=False
    )
```

```python
import functools
import math

import jax
import jax.numpy as jnp
from jax import lax
from jax.experimental import pallas as pl
from jax.experimental.pallas import tpu as pltpu
from jax.sharding import PartitionSpec as P


def solve_lower(lower_factor, target):
    return lax.linalg.triangular_solve(lower_factor, target, left_side=True, lower=True)


def general_body(
    prior_sample,
    measured_point_location,
    measured_data,
    measurement_noise_sigma,
    measured_slots_used,
):
    exact_arithmetic = lax.Precision.HIGHEST
    anomaly_matrix, points_in_region = prior_sample.shape
    region_batches = lax.axis_size("member")
    sample_total = anomaly_matrix * region_batches
    pointwise_spread = points_in_region // region_batches
    linear_position = measured_point_location.reshape(-1)
    obs_blk = linear_position.shape[0]
    observation_deviation = obs_blk // region_batches
    propagated_grid = jnp.take(prior_sample, linear_position, axis=1).reshape(
        anomaly_matrix, region_batches, observation_deviation
    )
    prior_regions = prior_sample.reshape(anomaly_matrix, region_batches, pointwise_spread)
    prior_sample_full, integrate_dynamics = (
        lax.all_to_all(prior_regions, "member", split_axis=1, concat_axis=0, tiled=True),
        lax.all_to_all(propagated_grid, "member", split_axis=1, concat_axis=0, tiled=True),
    )
    integrate_dynamics = integrate_dynamics.reshape(sample_total, observation_deviation)
    rank = lax.axis_index("member")
    start = rank * observation_deviation
    my_value = lax.dynamic_slice_in_dim(measured_data.reshape(-1), start, observation_deviation)
    my_sigma = lax.dynamic_slice_in_dim(
        measurement_noise_sigma.reshape(-1), start, observation_deviation
    )
    slots = start + jnp.arange(observation_deviation, dtype=jnp.int32)
    valid = slots < measured_slots_used[0]
    weight = jnp.where(valid, 1.0 / my_sigma, jnp.zeros_like(my_sigma))
    sim_mean = jnp.mean(integrate_dynamics, axis=0)
    perturbed = (integrate_dynamics - sim_mean[None, :]) * weight[None, :]
    innovation = (my_value - sim_mean) * weight
    gram_loc = jnp.dot(perturbed, perturbed.T, precision=exact_arithmetic)
    cross_loc = jnp.dot(perturbed, innovation, precision=exact_arithmetic)
    gram_block, cross_block = lax.psum((gram_loc, cross_loc), "member")
    gram_all, cross = lax.psum((gram_block, cross_block), "space")
    cov_matrix = gram_all + (sample_total - 1) * jnp.eye(sample_total, dtype=jnp.float32)
    lower_factor = jnp.linalg.cholesky(cov_matrix)
    inverse = solve_lower(lower_factor, jnp.eye(sample_total, dtype=jnp.float32))
    projected = jnp.dot(inverse, cross, precision=exact_arithmetic)
    mean_weight = jnp.dot(inverse.T, projected, precision=exact_arithmetic)
    weight_matrix_update = math.sqrt(sample_total - 1) * inverse + mean_weight[None, :]
    sample_vectors = prior_sample_full.reshape(sample_total, -1)
    prior_average = jnp.mean(sample_vectors, axis=0)
    updated_sample = prior_average[None, :] + jnp.dot(
        weight_matrix_update, sample_vectors - prior_average[None, :], precision=exact_arithmetic
    )
    returned = lax.all_to_all(
        updated_sample.reshape(prior_sample_full.shape),
        "member",
        split_axis=0,
        concat_axis=1,
        tiled=True,
    )
    return returned.reshape(anomaly_matrix, points_in_region)


MESH = pl.DeviceIdType.MESH
VMEM_SPEC = pl.BlockSpec(memory_space=pltpu.VMEM)
LANES = 128
MIB = 1 << 20
SUBLANES = 8


def split2(x):
    high = x.astype(jnp.bfloat16)
    low = (x - high.astype(jnp.float32)).astype(jnp.bfloat16)
    return high, low


def dot3(a, b, dims=((1,), (0,))):
    ah, al = split2(a)
    bh, bl = split2(b)
    d = functools.partial(
        lax.dot_general, dimension_numbers=(dims, ((), ())), preferred_element_type=jnp.float32
    )
    return (d(ah, bl) + d(al, bh)) + d(ah, bh)


def in_hbm(x):
    return pltpu.with_memory_space_constraint(x, pltpu.HBM)


def flat_row(ref):
    return jnp.concatenate([ref[i : i + 1, :] for i in range(ref.shape[0])], axis=1)


def gather_kernel(starts, x_ref, idx_ref, out_ref, *chunk_refs):
    step = pl.program_id(0)
    members, points = x_ref.shape
    shape = (SUBLANES, LANES)
    for (first, count), chunk_ref in zip(starts, chunk_refs):

        @pl.when((step >= first) & (step < first + count))
        def _(chunk_ref=chunk_ref):
            chunk_ref[...] = x_ref[...]

    for c in range(idx_ref.shape[0]):
        index = jnp.broadcast_to(idx_ref[c : c + 1, :], shape)
        lane = jnp.bitwise_and(index, LANES - 1)
        block = jnp.right_shift(index, LANES.bit_length() - 1) - step * (points // LANES)
        hits = [block == j for j in range(points // LANES)]
        columns = slice(c * LANES, (c + 1) * LANES)
        for g in range(0, members, SUBLANES):
            old = out_ref[g : g + SUBLANES, columns]
            got = jnp.where(step == 0, jnp.zeros(shape, jnp.float32), old)
            for j in range(points // LANES):
                x = x_ref[g : g + SUBLANES, j * LANES : (j + 1) * LANES]
                got = jnp.where(hits[j], jnp.take_along_axis(x, lane, axis=1), got)
            out_ref[g : g + SUBLANES, columns] = got


def gather_observed(prior, index, starts, tile):
    members, points = prior.shape
    slots = index.size
    f32 = jnp.float32
    return pl.pallas_call(
        functools.partial(gather_kernel, starts),
        grid=(points // tile,),
        out_shape=[jax.ShapeDtypeStruct((members, slots), f32)]
        + [jax.ShapeDtypeStruct((members, count * tile), f32) for _, count in starts],
        in_specs=[
            pl.BlockSpec((members, tile), lambda i: (0, i)),
            pl.BlockSpec(index.shape, lambda i: (0, 0)),
        ],
        out_specs=[pl.BlockSpec((members, slots), lambda i: (0, 0))]
        + [
            pl.BlockSpec(
                (members, tile),
                lambda i, first=first, count=count: (0, jnp.clip(i - first, 0, count - 1)),
            )
            for first, count in starts
        ],
        compiler_params=pltpu.CompilerParams(vmem_limit_bytes=12 * MIB),
        cost_estimate=pl.CostEstimate(
            flops=2 * members * slots * 256, bytes_accessed=16_000_000, transcendentals=0
        ),
    )(in_hbm(prior), in_hbm(index))


def send(src, dst, ssem, rsem, member, space):
    copy = pltpu.make_async_remote_copy(
        src_ref=src,
        dst_ref=dst,
        send_sem=ssem,
        recv_sem=rsem,
        device_id={"member": member, "space": space},
        device_id_type=MESH,
    )
    copy.start()
    return copy


def meet(devices):
    barrier = pltpu.get_barrier_semaphore()
    for member, space in devices:
        pl.semaphore_signal(
            barrier, inc=1, device_id={"member": member, "space": space}, device_id_type=MESH
        )
    pl.semaphore_wait(barrier, len(devices))


def neighbours():
    rank = lax.axis_index("member")
    return rank, rank + 1 - 2 * lax.rem(rank, 2), lax.rem(rank + 2, 4)


def exchange_kernel(ev_ref, out_ref, pair, ssem, rsem):
    rank, _, across = neighbours()
    place = lax.axis_index("space")
    rows = ev_ref.shape[0]
    meet([(across, place)])
    mine = pl.ds(pl.multiple_of((rank // 2) * rows, SUBLANES), rows)
    copy = send(ev_ref, pair.at[mine], ssem, rsem, across, place)
    pair[mine, :] = ev_ref[...]
    copy.wait()
    out_ref[...] = pair[...]


def exchange_observed(ev):
    rows, slots = ev.shape
    dma = pltpu.SemaphoreType.DMA
    pair = (rows * 2, slots)
    return pl.pallas_call(
        exchange_kernel,
        out_shape=jax.ShapeDtypeStruct(pair, jnp.float32),
        in_specs=[VMEM_SPEC],
        out_specs=VMEM_SPEC,
        scratch_shapes=[pltpu.VMEM(pair, jnp.float32), dma(()), dma(())],
        compiler_params=pltpu.CompilerParams(
            collective_id=0, has_side_effects=True, vmem_limit_bytes=4 * MIB
        ),
        cost_estimate=pl.CostEstimate(
            flops=1_000_000, bytes_accessed=20_000_000, transcendentals=0
        ),
    )(ev)


def gram_kernel(
    spaces,
    ev_ref,
    data_ref,
    sigma_ref,
    used_ref,
    out_ref,
    full,
    gram,
    parts,
    total,
    rs_send,
    rs_recv,
    ag_send,
    ag_recv,
    fin_send,
    fin_recv,
    ex_send,
    ex_recv,
):
    rank, side, _ = neighbours()
    place = lax.axis_index("space")
    half = lax.rem(rank, 2)
    samples, slots = full.shape
    rows = samples // 2
    group = samples // 4
    chunk = rows // spaces
    meet([(side, place)] + [(rank, lax.rem(place + d, spaces)) for d in range(1, spaces)])

    shared = []
    for i in range(2):
        source = ev_ref.at[pl.ds(i * group, group)]
        target = full.at[pl.ds(pl.multiple_of((half + 2 * i) * group, SUBLANES), group)]
        shared.append(send(source, target, ex_send.at[i], ex_recv.at[i], side, place))
    for i in range(2):
        own = pl.ds(pl.multiple_of((half + 2 * i) * group, SUBLANES), group)
        full[own, :] = ev_ref[i * group : (i + 1) * group, :]
    slot = lax.broadcasted_iota(jnp.int32, (1, slots), 1)
    weight = jnp.where(slot < used_ref[0], 1.0 / flat_row(sigma_ref), 0.0)
    for copy in shared:
        copy.wait_recv()
    ev = full[...]
    mean = jnp.sum(ev, axis=0, keepdims=True) * (1.0 / samples)
    anomalies = (ev - mean) * weight
    innovation = (flat_row(data_ref) - mean) * weight
    first = lax.broadcasted_iota(jnp.int32, (LANES, slots), 0) == 0
    extra = jnp.where(first, jnp.broadcast_to(innovation, (LANES, slots)), 0.0)
    mine = (full[pl.ds(pl.multiple_of(half * rows, SUBLANES), rows), :] - mean) * weight
    right = jnp.concatenate([anomalies, extra], axis=0)
    gram[...] = dot3(mine, right, ((1,), (1,)))

    copies = []
    for d in range(1, spaces):
        other = lax.rem(place + d, spaces)
        copies.append(
            send(
                gram.at[pl.ds(pl.multiple_of(other * chunk, SUBLANES), chunk)],
                parts.at[d - 1],
                rs_send.at[d - 1],
                rs_recv.at[d - 1],
                rank,
                other,
            )
        )
    acc = gram[pl.ds(pl.multiple_of(place * chunk, SUBLANES), chunk), :]
    for d in range(1, spaces):
        copies[d - 1].wait_recv()
        acc = acc + parts[d - 1]
    piece = pl.ds(pl.multiple_of(half * rows + place * chunk, SUBLANES), chunk)
    total[piece, :] = acc
    spread = []
    for d in range(1, spaces):
        other = lax.rem(place + d, spaces)
        spread.append(
            send(
                total.at[piece], total.at[piece], ag_send.at[d - 1], ag_recv.at[d - 1], rank, other
            )
        )
    for copy in spread:
        copy.wait_recv()
    mine_rows = total.at[pl.ds(pl.multiple_of(half * rows, SUBLANES), rows)]
    last = send(mine_rows, mine_rows, fin_send, fin_recv, side, place)
    last.wait_recv()
    for copy in (*shared, *copies, *spread, last):
        copy.wait_send()
    out_ref[...] = total[...]


def summed_gram(ev, data, sigma, used, spaces):
    rows, slots = ev.shape
    samples = rows * 2
    width = samples + LANES
    dma = pltpu.SemaphoreType.DMA
    return pl.pallas_call(
        functools.partial(gram_kernel, spaces),
        out_shape=jax.ShapeDtypeStruct((samples, width), jnp.float32),
        in_specs=[VMEM_SPEC] * 3 + [pl.BlockSpec(memory_space=pltpu.SMEM)],
        out_specs=VMEM_SPEC,
        scratch_shapes=[
            pltpu.VMEM((samples, slots), jnp.float32),
            pltpu.VMEM((rows, width), jnp.float32),
            pltpu.VMEM((spaces - 1, rows // spaces, width), jnp.float32),
            pltpu.VMEM((samples, width), jnp.float32),
            dma((spaces - 1,)),
            dma((spaces - 1,)),
            dma((spaces - 1,)),
            dma((spaces - 1,)),
            dma(()),
            dma(()),
            dma((2,)),
            dma((2,)),
        ],
        compiler_params=pltpu.CompilerParams(collective_id=1, has_side_effects=True, vmem_limit_bytes=16 * MIB),
        cost_estimate=pl.CostEstimate(
            flops=4_000_000, bytes_accessed=6_000_000, transcendentals=0
        ),
    )(ev, data, sigma, used)


PIVOTS = 4


def inverse_factor(a):
    size = a.shape[0]
    count = size // SUBLANES
    shape = (SUBLANES, size)
    m = [a[SUBLANES * i : SUBLANES * (i + 1), :] for i in range(count)]
    diag = [None] * count
    lane = lax.broadcasted_iota(jnp.int32, shape, 1)
    sub = lax.broadcasted_iota(jnp.int32, shape, 0)

    def column(x, k):
        return jnp.broadcast_to(x[:, k : k + 1], shape)

    def row(x, r):
        return jnp.broadcast_to(x[r : r + 1, :], shape)

    for k in range(0, size, PIVOTS):
        t, r = divmod(k, SUBLANES)
        inside = (lane >= k) & (lane < k + PIVOTS)
        cols = [column(m[t], k + q) for q in range(PIVOTS)]
        pivot = {(q, p): row(cols[p], r + q) for p in range(PIVOTS) for q in range(p, PIVOTS)}
        base = [
            jnp.where(inside, jnp.where(lane == k + q, 1.0, 0.0), row(m[t], r + q))
            for q in range(PIVOTS)
        ]
        inverse = []
        for p in range(PIVOTS):
            inverse.append(1.0 / pivot[p, p])
            for q in range(p + 1, PIVOTS):
                factor = pivot[q, p] * inverse[p]
                base[q] = base[q] - factor * base[p]
                for s in range(q, PIVOTS):
                    pivot[s, q] = pivot[s, q] - factor * pivot[s, p]
        for p in range(PIVOTS):
            old = diag[t]
            diag[t] = pivot[p, p] if old is None else jnp.where(sub >= r + p, pivot[p, p], old)
        for i in range(t, count):
            cols_i = cols if i == t else [column(m[i], k + q) for q in range(PIVOTS)]
            cols_i = list(cols_i)
            if i == t:
                unit = jnp.where(lane - k == sub - r, 1.0, 0.0)
                x = jnp.where(inside & (sub >= r), unit, m[i])
            else:
                x = jnp.where(inside, 0.0, m[i])
            for p in range(PIVOTS):
                mult = cols_i[p] * inverse[p]
                if i == t:
                    mult = jnp.where(sub > r + p, mult, 0.0)
                for q in range(p + 1, PIVOTS):
                    cols_i[q] = cols_i[q] - mult * pivot[q, p]
                x = x - mult * base[p]
            m[i] = x
    out = []
    for i in range(count):
        keep = lane <= sub + SUBLANES * i
        out.append(jnp.where(keep, m[i] * lax.rsqrt(diag[i]), 0.0))
    return jnp.concatenate(out, axis=0)


def eye_mask(rows, cols):
    shape = (rows, cols)
    return lax.broadcasted_iota(jnp.int32, shape, 0) == lax.broadcasted_iota(jnp.int32, shape, 1)


def transform_kernel(g_ref, out_ref, inv_ref):
    samples = g_ref.shape[0]
    b = LANES
    ridge = float(samples - 1)
    n = samples // b
    work = {}
    for i in range(n):
        for j in range(i + 1):
            block = g_ref[i * b : (i + 1) * b, j * b : (j + 1) * b]
            work[i, j] = block + jnp.where(eye_mask(b, b), ridge, 0.0) if i == j else block
    inv = {}
    low = {}
    for k in range(n):
        inv[k, k] = inverse_factor(work[k, k])
        for i in range(k + 1, n):
            low[i, k] = dot3(work[i, k], inv[k, k], ((1,), (1,)))
        for i in range(k + 1, n):
            for j in range(k + 1, i + 1):
                work[i, j] = work[i, j] - dot3(low[i, k], low[j, k], ((1,), (1,)))
        for j in range(k):
            acc = dot3(low[k, j], inv[j, j])
            for s in range(j + 1, k):
                acc = acc + dot3(low[k, s], inv[s, j])
            inv[k, j] = -dot3(inv[k, k], acc)
    zero = jnp.zeros((b, b), jnp.float32)
    full = jnp.concatenate(
        [
            jnp.concatenate([inv[i, j] if j <= i else zero for j in range(n)], axis=1)
            for i in range(n)
        ],
        axis=0,
    )
    inv_ref[...] = full
    cross = g_ref[:, samples : samples + b]
    projected = dot3(full, cross)
    mean_weight = jnp.sum(full * projected[:, 0:1], axis=0, keepdims=True)
    out_ref[...] = math.sqrt(samples - 1) * full + mean_weight


def transform_of(gram):
    samples = gram.shape[0]
    return pl.pallas_call(
        transform_kernel,
        out_shape=jax.ShapeDtypeStruct((samples, samples), jnp.float32),
        in_specs=[VMEM_SPEC],
        out_specs=VMEM_SPEC,
        scratch_shapes=[pltpu.VMEM((samples, samples), jnp.float32)],
        compiler_params=pltpu.CompilerParams(vmem_limit_bytes=8 * MIB),
        cost_estimate=pl.CostEstimate(
            flops=4_000_000, bytes_accessed=4_000_000, transcendentals=0
        ),
    )(gram)


def analysis_kernel(t_ref, own_ref, side_ref, across_ref, both_ref, out_ref, x_ref):
    rank = lax.axis_index("member")
    rows = own_ref.shape[0]
    samples = x_ref.shape[0]
    side = rank + 1 - 2 * lax.rem(rank, 2)
    across = lax.rem(rank + 2, 4)
    both = lax.rem(side + 2, 4)
    pieces = ((rank, own_ref), (side, side_ref), (across, across_ref), (both, both_ref))
    total = None
    for member, ref in pieces:
        part = jnp.sum(ref[...], axis=0, keepdims=True)
        total = part if total is None else total + part
    mean = total * (1.0 / samples)
    for member, ref in pieces:
        x_ref[pl.ds(pl.multiple_of(member * rows, SUBLANES), rows), :] = ref[...] - mean
    mine = t_ref[pl.ds(pl.multiple_of(rank * rows, SUBLANES), rows), :]
    th, tl = split2(mine)
    xh, xl = split2(x_ref[...])
    dot = functools.partial(jnp.dot, preferred_element_type=jnp.float32)
    both_parts = dot(jnp.concatenate([th, tl], axis=0), xh)
    out_ref[...] = mean + ((both_parts[rows:] + dot(th, xl)) + both_parts[:rows])


def analysis_chunk(transform, own, pieces, first, out, tile=1024):
    rows, points = own.shape
    samples = transform.shape[0]
    whole = pl.BlockSpec((samples, samples), lambda i: (0, 0))
    placed = pl.BlockSpec((rows, tile), lambda i: (0, i + first))
    block = pl.BlockSpec((rows, tile), lambda i: (0, i))
    kernel, extra, specs, alias = analysis_kernel, (), [], {}
    if out is not None:
        kernel = lambda t, o, s, a, b, _, *rest: analysis_kernel(t, o, s, a, b, *rest)
        extra, specs, alias = (out,), [pl.BlockSpec(memory_space=pl.ANY)], {5: 0}
    return pl.pallas_call(
        kernel,
        grid=(pieces[1].shape[1] // tile,),
        out_shape=jax.ShapeDtypeStruct((rows, points), jnp.float32),
        in_specs=[whole, placed, placed] + [block] * 2 + specs,
        out_specs=placed,
        scratch_shapes=[pltpu.VMEM((samples, tile), jnp.float32)],
        input_output_aliases=alias,
        compiler_params=pltpu.CompilerParams(vmem_limit_bytes=12 * MIB),
    )(transform, own, *pieces, *extra)


TILE = 1024
EIGHTHS = (1, 4, 2, 1)


def body(*arrays):
    prior_sample = arrays[0]
    rows, points = prior_sample.shape
    members, spaces = lax.axis_size("member"), lax.axis_size("space")
    if (
        members != 4
        or rows * members % (2 * SUBLANES * spaces)
        or rows * members % LANES
        or rows % SUBLANES
        or points % (8 * TILE)
    ):
        return general_body(*arrays)
    return fast_body(members, spaces, *arrays)


def fast_body(members, spaces, prior_sample, location, data, sigma, used):
    points = prior_sample.shape[1]
    near = [(i, i ^ 1) for i in range(members)]
    far = [(i, i ^ 2) for i in range(members)]
    counts = [e * points // (8 * TILE) for e in EIGHTHS]
    starts = [(sum(counts[:i]), n) for i, n in enumerate(counts)]
    across = [lax.ppermute(prior_sample[:, : counts[0] * TILE], "member", far)]
    side = lax.ppermute(prior_sample, "member", near)
    observed, *chunks = gather_observed(prior_sample, location, starts[1:], TILE)
    gathered = exchange_observed(observed)
    *chunks, gathered = lax.optimization_barrier((*chunks, gathered))
    for chunk in chunks:
        across.append(lax.ppermute(chunk, "member", far))
    gram = summed_gram(gathered, data, sigma, used, spaces)
    across[0], gram = lax.optimization_barrier((across[0], gram))
    both = lax.ppermute(across[0], "member", near)
    out = transform = transform_of(gram)
    result = None
    for i, (first, _) in enumerate(starts):
        now = both
        if 0 < i < len(starts) - 1:
            both = lax.ppermute(across[i + 1], "member", near)
        elif i + 1 < len(starts):
            across[i + 1], out = lax.optimization_barrier((across[i + 1], out))
            if i == 0:
                transform = out
            else:
                result = out
            both = lax.ppermute(across[i + 1], "member", near)
        result = analysis_chunk(
            transform, prior_sample, (side, across[i], now), first, result
        )
        out = result
    return result


def solution(mesh):
    placed = (
        P("member", "space"),
        P("space", None),
        P("space", None),
        P("space", None),
        P("space"),
    )
    return jax.shard_map(
        body, mesh=mesh, in_specs=placed, out_specs=P("member", "space"), check_vma=False
    )
```
